32 devices in a mesh: ctx: 4 (over z), tp: 8 (over y, x, core).
Axes of the slice: x: 2, y: 2, z: 4, core: 2. Of those that a mesh axis runs over, the one named last changes fastest.
Arguments:
- hidden_in: bfloat16 [2, 1024, 4096], P(None, 'ctx', 'tp'), may hold values from -6 to 6
- decode_in: bfloat16 [2, 4096], replicated, may hold values from -6 to 6
- pre_len: int32 [2], replicated, may hold values from 1 to 2048, as said below
- new_len: int32 [2], replicated, may hold values from 1 to 1024, as said below
- key_cache: bfloat16 [2, 2048, 4096], P(None, 'ctx', 'tp'), may hold values from -120 to 120
- value_cache: bfloat16 [2, 2048, 4096], P(None, 'ctx', 'tp'), may hold values from -6 to 6
- ln_attn_gain: float32 [4096], replicated, may hold values from 0.1 to 1.9
- ln_attn_bias: float32 [4096], replicated, may hold values from -1.5 to 1.5
- ln_mlp_gain: float32 [4096], replicated, may hold values from 0.1 to 1.9
- ln_mlp_bias: float32 [4096], replicated, may hold values from -1.5 to 1.5
- qkv_weight: bfloat16 [3, 4096, 4096], P(None, None, 'tp'), may hold values from -0.09375 to 0.09375
- qkv_bias: float32 [3, 4096], P(None, 'tp'), may hold values from -1.5 to 1.5
- out_weight: bfloat16 [4096, 4096], P('tp'), may hold values from -0.09375 to 0.09375
- out_bias: float32 [4096], replicated, may hold values from -3 to 3
- up_weight: bfloat16 [4096, 12288], P(None, 'tp'), may hold values from -0.09375 to 0.09375
- up_bias: float32 [12288], P('tp'), may hold values from -3 to 3
- down_weight: bfloat16 [12288, 4096], P('tp'), may hold values from -0.0546875 to 0.0546875
- down_bias: float32 [4096], replicated, may hold values from -3 to 3
Outputs:
- prefill_out: bfloat16 [2, 1024, 4096], P(None, 'ctx', 'tp')
- new_keys: bfloat16 [2, 1024, 4096], P(None, 'ctx', 'tp')
- new_values: bfloat16 [2, 1024, 4096], P(None, 'ctx', 'tp')
- decode_out: bfloat16 [2, 4096], P(None, 'tp')
The draws below stay inside these ranges and needn't reach their ends.
Inputs may be any that keep to these rules, and one draw needn't show every extreme that they name: `pre_len`: one sequence has a full cached prefix of 2048 slots; the others are shorter. `new_len`: one sequence has a full new prompt of 1024 slots; the others are shorter.
All inputs are finite; a program needn't handle non-finite values.
Results may differ from the reference program's by a relative error of at most 0.012.
Values may be sent and summed in bfloat16 or wider, within the bound.
No kernel may reach another device: no remote copies, remote signals or barrier semaphores. Data moves between devices by JAX's collectives and lax.ppermute only.
A program may use at most 192 MiB of HBM per device.

```python
import math
import jax
import jax.numpy as jnp
from jax import lax

D = 4096
HEADS = 32
HD = 128
ROT = 32
FF = 12288
SEQS = 2
NEW = 1024
PRE = 2048


def draw_pre_len(key, part):
    first, second = jax.random.split(jax.random.fold_in(key, 11))
    lengths = jax.random.randint(first, (SEQS,), 1, PRE)
    pick = jax.random.randint(second, (), 0, SEQS)
    return jnp.where(jnp.arange(SEQS) == pick, PRE, lengths).astype(jnp.int32)


def draw_new_len(key, part):
    first, second = jax.random.split(jax.random.fold_in(key, 23))
    lengths = jax.random.randint(first, (SEQS,), 1, NEW)
    pick = jax.random.randint(second, (), 0, SEQS)
    return jnp.where(jnp.arange(SEQS) == pick, NEW, lengths).astype(jnp.int32)


def bias_table(key):
    parts = jax.random.split(jax.random.fold_in(key, 5), 3)
    small = jnp.clip(jax.random.normal(parts[0], (3, HEADS, HD), jnp.float32) * 0.5, -1.5, 1.5)
    size = jax.random.uniform(parts[1], (HEADS, HD), jnp.float32, 0.2, 0.3)
    signs = jnp.where(jax.random.randint(parts[2], (HEADS, HD), 0, 2) == 1, 1.0, -1.0)
    upper = jnp.arange(HD) >= ROT
    query = jnp.where(upper[None, :], signs * size, 0.5 * small[0])
    return jnp.stack([query, small[1], small[2]], axis=0)


def draw_qkv_bias(key, part):
    return bias_table(key).reshape(3, HEADS * HD).astype(jnp.float32)


def draw_key_cache(key, part):
    keys = jax.random.split(jax.random.fold_in(key, 37), 7)
    shape = (SEQS, PRE, HEADS, HD)
    base = jnp.clip(2.0 * jax.random.normal(keys[0], shape, jnp.float32), -8.0, 8.0)
    upper = (jnp.arange(HD) >= ROT).astype(jnp.float32)
    pattern = jnp.sign(bias_table(key)[0]) * upper[None, :]
    pairs = PRE // 2
    hot = jax.random.randint(keys[1], (SEQS, pairs), 0, 24) == 0
    forced = jax.random.randint(keys[2], (SEQS, 1), 0, pairs)
    hot = hot | (jnp.arange(pairs)[None, :] == forced)
    hot = jnp.repeat(hot, 2, axis=1)
    head_hot = jax.random.randint(keys[3], (SEQS, HEADS), 0, 2) == 1
    head_pick = jax.random.randint(keys[4], (SEQS, 1), 0, HEADS)
    head_hot = head_hot | (jnp.arange(HEADS)[None, :] == head_pick)
    strength = jax.random.uniform(keys[5], (SEQS, pairs, HEADS), jnp.float32, 110.0, 240.0)
    gap = jax.random.uniform(keys[6], (SEQS, pairs, HEADS), jnp.float32, 1.0, 3.0)
    unit = math.sqrt(HD) / (0.25 * (HD - ROT))
    first_c = strength * unit
    second_c = first_c * (strength + gap) / strength
    level = jnp.stack([first_c, second_c], axis=2).reshape(SEQS, PRE, HEADS)
    strong = level[..., None] * pattern[None, None] + 0.1 * base
    chosen = hot[:, :, None, None] & head_hot[:, None, :, None] & (upper[None, None, None, :] > 0.5)
    values = jnp.clip(jnp.where(chosen, strong, base), -118.0, 118.0)
    return values.reshape(SEQS, PRE, HEADS * HD).astype(jnp.bfloat16)


def block_scale(own_key, extent, cuts, least, top_value):
    loudness = 1.0
    for dim, blocks in cuts:
        draws = jax.random.uniform(jax.random.fold_in(jax.random.fold_in(own_key, 6), dim), (blocks,), jnp.float32, least / len(cuts), top_value / len(cuts))
        loudness = loudness * jnp.repeat(jnp.exp(draws), extent[dim] // blocks).reshape((-1,) + (1,) * (len(extent) - 1 - dim))
    return loudness


def bell_draw(rng, shape, scale, reach, pieces=(), held_as=jnp.bfloat16):
    result = jax.random.normal(rng, shape, jnp.float32) * scale
    if len(pieces) > 0:
        result = block_scale(rng, shape, pieces, -0.22, 0.18) * result
    return jnp.clip(result, min=-reach, max=reach).astype(held_as)


def setup_inputs(seed: int = 0) -> dict:
    key_of = jax.random.split(jax.random.key(seed), 19)
    return {
        "hidden_in": bell_draw(key_of[0], (SEQS, NEW, D), 1.0, 6.0, ((1, 4), (2, 8))),
        "decode_in": bell_draw(key_of[1], (SEQS, D), 1.0, 6.0),
        "pre_len": draw_pre_len(jax.random.fold_in(key_of[18], 71), 0),
        "new_len": draw_new_len(jax.random.fold_in(key_of[18], 71), 0),
        "key_cache": draw_key_cache(jax.random.fold_in(key_of[18], 71), 0),
        "value_cache": bell_draw(key_of[5], (SEQS, PRE, HEADS * HD), 1.0, 6.0, ((1, 4), (2, 8))),
        "ln_attn_gain": jnp.clip(1.0 + 0.18 * jax.random.normal(key_of[6], (D,), jnp.float32), 0.1, 1.9),
        "ln_attn_bias": bell_draw(key_of[7], (D,), 0.3, 1.5, (), jnp.float32),
        "ln_mlp_gain": jnp.clip(1.0 + 0.18 * jax.random.normal(key_of[8], (D,), jnp.float32), 0.1, 1.9),
        "ln_mlp_bias": bell_draw(key_of[9], (D,), 0.3, 1.5, (), jnp.float32),
        "qkv_weight": bell_draw(key_of[10], (3, D, HEADS * HD), D ** -0.5, 0.09375, ((2, 8),)),
        "qkv_bias": draw_qkv_bias(jax.random.fold_in(key_of[18], 71), 0),
        "out_weight": bell_draw(key_of[12], (HEADS * HD, D), (HEADS * HD) ** -0.5, 0.09375, ((0, 8),)),
        "out_bias": bell_draw(key_of[13], (D,), 0.5, 3.0, (), jnp.float32),
        "up_weight": bell_draw(key_of[14], (D, FF), D ** -0.5, 0.09375, ((1, 8),)),
        "up_bias": bell_draw(key_of[15], (FF,), 0.5, 3.0, ((0, 8),), jnp.float32),
        "down_weight": bell_draw(key_of[16], (FF, D), FF ** -0.5, 0.0546875, ((0, 8),)),
        "down_bias": bell_draw(key_of[17], (D,), 0.5, 3.0, (), jnp.float32),
    }


EPS = 1e-05
NEG = -1e+30

def norm_rows(rows, gain, shift):
    values = rows.astype(jnp.float32)
    center = values - lax.optimization_barrier(jnp.mean(values, axis=-1, keepdims=True))
    spread = lax.optimization_barrier(jnp.mean(center * center, axis=-1, keepdims=True))
    return (center * lax.rsqrt(spread + EPS) * gain + shift).astype(jnp.bfloat16)

def rotate(values, position):
    half = ROT // 2
    freqs = jnp.exp(jnp.arange(half, dtype=jnp.float32) * (-2.0 * math.log(10000.0) / ROT))
    angle = position.astype(jnp.float32)[..., None] * freqs
    cosine = jnp.cos(angle)
    sine = jnp.sin(angle)
    first = values[..., :half]
    second = values[..., half:ROT]
    return jnp.concatenate([first * cosine - second * sine, second * cosine + first * sine, values[..., ROT:]], axis=-1)

def rounded(values):
    return lax.optimization_barrier(values.astype(jnp.bfloat16)).astype(jnp.float32)

def reference(hidden_in, decode_in, pre_len, new_len, key_cache, value_cache, ln_attn_gain, ln_attn_bias, ln_mlp_gain, ln_mlp_bias, qkv_weight, qkv_bias, out_weight, out_bias, up_weight, up_bias, down_weight, down_bias):
    cols = HEADS * HD
    rows_new = SEQS * NEW
    scale = 1.0 / math.sqrt(HD)
    joined = jnp.concatenate([hidden_in.reshape(rows_new, D), decode_in], axis=0)
    attn_in = norm_rows(joined, ln_attn_gain, ln_attn_bias)
    mlp_in = norm_rows(joined, ln_mlp_gain, ln_mlp_bias)
    proj = [jnp.dot(attn_in, qkv_weight[i], preferred_element_type=jnp.float32) + qkv_bias[i] for i in range(3)]
    up_act = jax.nn.gelu(jnp.dot(mlp_in, up_weight, preferred_element_type=jnp.float32) + up_bias, approximate=False).astype(jnp.bfloat16)
    mlp_part = jnp.dot(up_act, down_weight, preferred_element_type=jnp.float32)
    new_index = jnp.arange(NEW, dtype=jnp.int32)
    position = pre_len[:, None] + new_index[None, :]
    dec_position = pre_len + new_len
    q_new = rotate(proj[0][:rows_new].reshape(SEQS, NEW, HEADS, HD), position[..., None]).astype(jnp.bfloat16)
    k_new = rotate(proj[1][:rows_new].reshape(SEQS, NEW, HEADS, HD), position[..., None]).astype(jnp.bfloat16)
    v_new = proj[2][:rows_new].reshape(SEQS, NEW, HEADS, HD).astype(jnp.bfloat16)
    q_dec = rotate(proj[0][rows_new:].reshape(SEQS, HEADS, HD), dec_position[:, None]).astype(jnp.bfloat16)
    k_dec = rotate(proj[1][rows_new:].reshape(SEQS, HEADS, HD), dec_position[:, None]).astype(jnp.bfloat16)
    v_dec = proj[2][rows_new:].reshape(SEQS, HEADS, HD).astype(jnp.bfloat16)
    live = new_index[None, :] < new_len[:, None]
    new_keys = jnp.where(live[..., None], k_new.reshape(SEQS, NEW, cols), 0).astype(jnp.bfloat16)
    new_values = jnp.where(live[..., None], v_new.reshape(SEQS, NEW, cols), 0).astype(jnp.bfloat16)
    keys_all = jnp.concatenate([key_cache.reshape(SEQS, PRE, HEADS, HD), k_new], axis=1)
    values_all = jnp.concatenate([value_cache.reshape(SEQS, PRE, HEADS, HD), v_new], axis=1)
    key_pos = jnp.arange(PRE + NEW, dtype=jnp.int32)
    is_prefix = key_pos < PRE
    new_pos = key_pos - PRE
    prefix_ok = is_prefix[None, :] & (key_pos[None, :] < pre_len[:, None])
    new_ok = jnp.logical_not(is_prefix)[None, :] & (new_pos[None, :] < new_len[:, None])

    def one_pair(item):
        queries, keys, values, pre_row, new_row = item
        scores = jnp.dot(queries, keys.T, preferred_element_type=jnp.float32) * scale
        allowed = pre_row[None, :] | new_row[None, :] & (new_pos[None, :] <= new_index[:, None])
        scores = jnp.where(allowed, scores, NEG)
        top = lax.optimization_barrier(jnp.max(scores, axis=1, keepdims=True))
        weight = jnp.where(allowed, jnp.exp(scores - top), 0.0)
        total = lax.optimization_barrier(jnp.sum(weight, axis=1, keepdims=True))
        acc = jnp.dot(weight.astype(jnp.bfloat16), values, preferred_element_type=jnp.float32)
        return acc / total
    flat_q = q_new.transpose(0, 2, 1, 3).reshape(SEQS * HEADS, NEW, HD)
    flat_k = keys_all.transpose(0, 2, 1, 3).reshape(SEQS * HEADS, PRE + NEW, HD)
    flat_v = values_all.transpose(0, 2, 1, 3).reshape(SEQS * HEADS, PRE + NEW, HD)
    flat_pre = jnp.repeat(prefix_ok, HEADS, axis=0)
    flat_new = jnp.repeat(new_ok, HEADS, axis=0)
    heads_out = lax.map(one_pair, (flat_q, flat_k, flat_v, flat_pre, flat_new))
    attn_new = heads_out.reshape(SEQS, HEADS, NEW, HD).transpose(0, 2, 1, 3).reshape(rows_new, cols).astype(jnp.bfloat16)
    dec_scores = jnp.einsum('shd,skhd->shk', q_dec.astype(jnp.float32), keys_all.astype(jnp.float32), precision=lax.Precision.HIGHEST) * scale
    dec_ok = (prefix_ok | new_ok)[:, None, :]
    dec_scores = jnp.where(dec_ok, dec_scores, NEG)
    own = lax.optimization_barrier(jnp.sum(q_dec.astype(jnp.float32) * k_dec.astype(jnp.float32), axis=-1)) * scale
    best = jnp.maximum(lax.optimization_barrier(jnp.max(dec_scores, axis=-1)), own)
    weight = jnp.where(dec_ok, jnp.exp(dec_scores - best[..., None]), 0.0)
    own_weight = jnp.exp(own - best)
    total = lax.optimization_barrier(jnp.sum(weight, axis=-1)) + own_weight
    acc = jnp.einsum('shk,skhd->shd', rounded(weight), values_all.astype(jnp.float32), precision=lax.Precision.HIGHEST)
    acc = acc + rounded(own_weight)[..., None] * v_dec.astype(jnp.float32)
    attn_dec = (acc / total[..., None]).reshape(SEQS, cols).astype(jnp.bfloat16)
    attn_rows = jnp.concatenate([attn_new, attn_dec], axis=0)
    branches = jnp.dot(attn_rows, out_weight, preferred_element_type=jnp.float32) + mlp_part
    bias = out_bias + down_bias
    prefill = hidden_in.astype(jnp.float32) + branches[:rows_new].reshape(SEQS, NEW, D) + bias
    prefill_out = jnp.where(live[..., None], prefill, 0.0).astype(jnp.bfloat16)
    decode_out = (decode_in.astype(jnp.float32) + branches[rows_new:] + bias).astype(jnp.bfloat16)
    return (prefill_out, new_keys, new_values, decode_out)
```

```python
import functools
import math

import jax
import jax.numpy as jnp
from jax import lax
from jax.experimental import pallas as pl
from jax.experimental.pallas import tpu as pltpu
from jax.sharding import PartitionSpec as P

HD = 128
ROT = 32


EPS = 1e-05
NEG = -1e30


def joined_2(part, axis, combine):
    gathered = jax.tree.map(lambda a: lax.all_gather(a, axis), part)

    def take(source):
        return jax.tree.map(lambda a: lax.dynamic_index_in_dim(a, source, 0, False), gathered)

    return lax.fori_loop(
        1, lax.axis_size(axis), lambda source, state: combine(state, take(source)), take(0)
    )


def norm_rows(rows, gain, shift):
    values = rows.astype(jnp.float32)
    center = values - jnp.mean(values, axis=-1, keepdims=True)
    spread = jnp.mean(center * center, axis=-1, keepdims=True)
    return (center * lax.rsqrt(spread + EPS) * gain + shift).astype(jnp.bfloat16)


def rotate(values, position):
    half = ROT // 2
    freqs = jnp.exp(jnp.arange(half, dtype=jnp.float32) * (-2.0 * math.log(10000.0) / ROT))
    angle = position.astype(jnp.float32)[..., None] * freqs
    cosine = jnp.cos(angle)
    sine = jnp.sin(angle)
    first = values[..., :half]
    second = values[..., half:ROT]
    return jnp.concatenate(
        [first * cosine - second * sine, second * cosine + first * sine, values[..., ROT:]], axis=-1
    )


def key_status(first, count, pre_dev, new_dev, pre_len, new_len):
    index = first + jnp.arange(count, dtype=jnp.int32)
    owner = index // (pre_dev + new_dev)
    offset = index % (pre_dev + new_dev)
    is_prefix = offset < pre_dev
    prefix_pos = owner * pre_dev + offset
    new_pos = owner * new_dev + offset - pre_dev
    prefix_ok = is_prefix[None, :] & (prefix_pos[None, :] < pre_len[:, None])
    new_ok = jnp.logical_not(is_prefix)[None, :] & (new_pos[None, :] < new_len[:, None])
    return (prefix_ok, new_ok, new_pos)


def absorb(state, queries, keys, values, allowed):
    top, total, acc = state
    scores = jnp.einsum("sqhd,skhd->shqk", queries, keys, preferred_element_type=jnp.float32) * (
        1.0 / math.sqrt(HD)
    )
    mask = allowed[:, None]
    scores = jnp.where(mask, scores, NEG)
    new_top = jnp.maximum(top, jnp.max(scores, axis=-1))
    weight = jnp.where(mask, jnp.exp(scores - new_top[..., None]), 0.0)
    factor = jnp.exp(top - new_top)
    total = total * factor + jnp.sum(weight, axis=-1)
    acc = acc * factor[..., None] + jnp.einsum(
        "shqk,skhd->shqd", weight.astype(jnp.bfloat16), values, preferred_element_type=jnp.float32
    )
    return (new_top, total, acc)


def empty_state(seqs, heads_dev, count):
    return (
        jnp.full((seqs, heads_dev, count), NEG, jnp.float32),
        jnp.zeros((seqs, heads_dev, count), jnp.float32),
        jnp.zeros((seqs, heads_dev, count, HD), jnp.float32),
    )


def join_parts(first, second):
    best = jnp.maximum(first[0], second[0])
    left = jnp.exp(first[0] - best)
    right = jnp.exp(second[0] - best)
    return (
        best,
        first[1] * left + second[1] * right,
        first[2] * left[..., None] + second[2] * right[..., None],
    )


def shards(
    hidden_in,
    decode_in,
    pre_len,
    new_len,
    key_cache,
    value_cache,
    ln_attn_gain,
    ln_attn_bias,
    ln_mlp_gain,
    ln_mlp_bias,
    qkv_weight,
    qkv_bias,
    out_weight,
    out_bias,
    up_weight,
    up_bias,
    down_weight,
    down_bias,
):
    seqs, new_dev, part_cols = hidden_in.shape
    pre_dev = key_cache.shape[1]
    local_cols = qkv_weight.shape[2]
    heads_dev = local_cols // HD
    width = decode_in.shape[1]
    block_len = pre_dev + new_dev
    rows_new = seqs * new_dev
    ctx_rank = lax.axis_index("ctx")
    tp_rank = lax.axis_index("tp")
    whole = lax.all_gather(hidden_in, "tp", axis=2, tiled=True)
    joined = jnp.concatenate([whole.reshape(rows_new, width), decode_in], axis=0)
    attn_in = norm_rows(joined, ln_attn_gain, ln_attn_bias)
    mlp_in = norm_rows(joined, ln_mlp_gain, ln_mlp_bias)
    proj = [
        jnp.dot(attn_in, qkv_weight[i], preferred_element_type=jnp.float32) + qkv_bias[i]
        for i in range(3)
    ]
    up_act = jax.nn.gelu(
        jnp.dot(mlp_in, up_weight, preferred_element_type=jnp.float32) + up_bias, approximate=False
    ).astype(jnp.bfloat16)
    query_index = ctx_rank * new_dev + jnp.arange(new_dev, dtype=jnp.int32)
    position = pre_len[:, None] + query_index[None, :]
    dec_position = pre_len + new_len
    q_new = rotate(
        proj[0][:rows_new].reshape(seqs, new_dev, heads_dev, HD), position[..., None]
    ).astype(jnp.bfloat16)
    k_new = rotate(
        proj[1][:rows_new].reshape(seqs, new_dev, heads_dev, HD), position[..., None]
    ).astype(jnp.bfloat16)
    v_new = proj[2][:rows_new].reshape(seqs, new_dev, heads_dev, HD).astype(jnp.bfloat16)
    q_dec = rotate(proj[0][rows_new:].reshape(seqs, heads_dev, HD), dec_position[:, None]).astype(
        jnp.bfloat16
    )
    k_dec = rotate(proj[1][rows_new:].reshape(seqs, heads_dev, HD), dec_position[:, None]).astype(
        jnp.bfloat16
    )
    v_dec = proj[2][rows_new:].reshape(seqs, heads_dev, HD).astype(jnp.bfloat16)
    live = query_index[None, :] < new_len[:, None]
    flat_keys = k_new.reshape(seqs, new_dev, local_cols)
    flat_values = v_new.reshape(seqs, new_dev, local_cols)
    new_keys = jnp.where(live[..., None], flat_keys, 0)
    new_values = jnp.where(live[..., None], flat_values, 0)
    local_block = jnp.concatenate(
        [jnp.stack([key_cache, value_cache], axis=2), jnp.stack([flat_keys, flat_values], axis=2)],
        axis=1,
    )
    local_keys = local_block[:, :, 0].reshape(seqs, block_len, heads_dev, HD)
    local_values = local_block[:, :, 1].reshape(seqs, block_len, heads_dev, HD)

    def allowed_for(first, count, queries_at):
        prefix_ok, new_ok, new_pos = key_status(first, count, pre_dev, new_dev, pre_len, new_len)
        return prefix_ok[:, None, :] | new_ok[:, None, :] & (
            new_pos[None, None, :] <= queries_at[None, :, None]
        )

    state = empty_state(seqs, heads_dev, new_dev)
    piece = lax.all_gather(local_block, "ctx", axis=1, tiled=True)
    blocks = piece.shape[1] // block_len

    def one_block(inner, number):
        begin = number * block_len
        slab = lax.dynamic_slice_in_dim(piece, begin, block_len, 1)
        keys = slab[:, :, 0].reshape(seqs, block_len, heads_dev, HD)
        values = slab[:, :, 1].reshape(seqs, block_len, heads_dev, HD)
        allowed = allowed_for(begin, block_len, query_index)
        return (absorb(inner, q_new, keys, values, allowed), None)

    state, _ = lax.scan(one_block, state, jnp.arange(blocks, dtype=jnp.int32))
    top, total, acc = state
    attn_new = (
        (acc / total[..., None])
        .transpose(0, 2, 1, 3)
        .reshape(rows_new, local_cols)
        .astype(jnp.bfloat16)
    )
    prefix_ok, new_ok, new_pos = key_status(
        ctx_rank * block_len, block_len, pre_dev, new_dev, pre_len, new_len
    )
    dec_allowed = (prefix_ok | new_ok)[:, None, :]
    dec_state = absorb(
        empty_state(seqs, heads_dev, 1), q_dec[:, None], local_keys, local_values, dec_allowed
    )
    dec_top, dec_total, dec_acc = joined_2(dec_state, "ctx", join_parts)
    dec_top = dec_top[..., 0]
    dec_total = dec_total[..., 0]
    dec_acc = dec_acc[:, :, 0]
    own = jnp.einsum("shd,shd->sh", q_dec, k_dec, preferred_element_type=jnp.float32) * (
        1.0 / math.sqrt(HD)
    )
    best = jnp.maximum(dec_top, own)
    far_factor = jnp.exp(dec_top - best)
    own_weight = jnp.exp(own - best)
    dec_total = dec_total * far_factor + own_weight
    dec_acc = dec_acc * far_factor[..., None] + jnp.einsum(
        "sh,shd->shd", own_weight.astype(jnp.bfloat16), v_dec, preferred_element_type=jnp.float32
    )
    attn_dec = (dec_acc / dec_total[..., None]).reshape(seqs, local_cols).astype(jnp.bfloat16)
    attn_rows = jnp.concatenate([attn_new, attn_dec], axis=0)
    branches = jnp.dot(attn_rows, out_weight, preferred_element_type=jnp.float32) + jnp.dot(
        up_act, down_weight, preferred_element_type=jnp.float32
    )
    summed_new, summed_dec = (
        lax.psum_scatter(
            branches[:rows_new].reshape(seqs, new_dev, width).astype(jnp.bfloat16),
            "tp",
            scatter_dimension=2,
            tiled=True,
        ).astype(jnp.float32),
        lax.psum_scatter(
            branches[rows_new:].astype(jnp.bfloat16), "tp", scatter_dimension=1, tiled=True
        ).astype(jnp.float32),
    )
    bias = lax.dynamic_slice_in_dim(out_bias + down_bias, tp_rank * part_cols, part_cols)
    prefill = hidden_in.astype(jnp.float32) + summed_new + bias
    prefill_out = jnp.where(live[..., None], prefill, 0.0).astype(jnp.bfloat16)
    dec_resid = lax.dynamic_slice_in_dim(decode_in, tp_rank * part_cols, part_cols, 1)
    decode_out = (dec_resid.astype(jnp.float32) + summed_dec + bias).astype(jnp.bfloat16)
    return (prefill_out, new_keys, new_values, decode_out)


BF = jnp.bfloat16
F32 = jnp.float32
DEC = 16
LSE = 16
SCALE = 1.0 / math.sqrt(HD)
VMEM = 56 * 1024 * 1024


def hop(value, axis, pairs):
    return lax.ppermute(value, axis, pairs)


def call(body, scal, ins, specs, outs, out_specs, grid, scratch=(), flops=0, nbytes=0):
    return pl.pallas_call(
        body,
        out_shape=outs,
        grid_spec=pltpu.PrefetchScalarGridSpec(
            num_scalar_prefetch=1,
            grid=grid,
            in_specs=specs,
            out_specs=out_specs,
            scratch_shapes=list(scratch),
        ),
        compiler_params=pltpu.CompilerParams(
            dimension_semantics=("arbitrary",) * len(grid), vmem_limit_bytes=VMEM
        ),
        cost_estimate=pl.CostEstimate(flops=flops, transcendentals=0, bytes_accessed=nbytes),
    )(scal, *ins)


def whole(shape):
    return pl.BlockSpec(tuple(shape), lambda i, sc: (0,) * len(shape))


def struct(shape, dtype):
    return jax.ShapeDtypeStruct(tuple(shape), dtype)


ME, RANK, LIMITS = 0, 1, 2


def turn(values, table, at):
    cosine, down, up = (table[i, pl.ds(0, values.shape[0]), :] for i in range(3))
    parts = []
    for h in range(values.shape[1] // HD):
        one = values[:, h * HD : (h + 1) * HD]
        parts.append(
            one * cosine
            + pltpu.roll(one, HD - ROT // 2, 1) * down
            + pltpu.roll(one, ROT // 2, 1) * up
        )
    return jnp.concatenate(parts, axis=1)


def query_body(rows, tail, part, sc, *refs):
    blocks = refs[:10]
    refs = refs[10:]
    dec = None
    if tail:
        dec, refs = refs[0], refs[1:]
    norms, weight, bias, table, q_out, attn_in, mlp_in = refs
    me = sc[ME]
    half = rows // 2
    width = part * 8

    def finish(values, base, count, cols):
        total = functools.reduce(lambda a, b: a + b, values)
        mean = jnp.sum(total, axis=-1, keepdims=True) * (1.0 / width)
        values = [v - mean for v in values]
        square = functools.reduce(lambda a, b: a + b, [v * v for v in values])
        spread = jnp.sum(square, axis=-1, keepdims=True) * (1.0 / width)
        inv = lax.rsqrt(spread + EPS)
        for v, col in zip(values, cols, strict=True):
            v = v * inv
            at = pl.ds(col, part)
            attn_in[pl.ds(base, count), at] = (
                v * norms[pl.ds(0, 1), at] + norms[pl.ds(1, 1), at]
            ).astype(BF)
            mlp_in[pl.ds(base, count), at] = (
                v * norms[pl.ds(2, 1), at] + norms[pl.ds(3, 1), at]
            ).astype(BF)

    @pl.when(pl.program_id(0) == 0)
    def _():
        cols = [pl.multiple_of((me ^ k) * part, part) for k in range(8)]
        for side in range(2):
            sources = [(blocks[k], side * half) for k in range(6)]
            sources += [(blocks[6 + side], 0), (blocks[8 + side], 0)]

            def step(i, carry):
                at = pl.multiple_of(i * 16, 16)
                values = [
                    ref[pl.ds(off + at, 16), :].astype(F32) for ref, off in sources
                ]
                finish(values, pl.multiple_of(side * half + at, 16), 16, cols)
                return carry

            lax.fori_loop(0, half // 16, step, 0)
        if tail:
            values = [dec[:, pl.ds(k * part, part)].astype(F32) for k in range(8)]
            finish(values, rows, tail, [k * part for k in range(8)])

    out = jnp.dot(attn_in[...], weight[0], preferred_element_type=F32) + bias[0]
    q_out[...] = turn(out, table, 0).astype(BF)


def queries(scal, blocks, dec, norms, weight, bias, table):
    rows, part = blocks[0].shape
    tail = 0 if dec is None else DEC
    width, cols = weight.shape[1:]
    tile = min(256, cols)
    total = rows + tail
    ins = [*blocks] + ([dec] if tail else []) + [norms, weight, bias, table]
    specs = [whole(b.shape) for b in blocks]
    if tail:
        specs.append(whole(dec.shape))
    specs += [
        whole(norms.shape),
        pl.BlockSpec((1, width, tile), lambda i, sc: (0, 0, i)),
        pl.BlockSpec((1, 1, tile), lambda i, sc: (0, 0, i)),
        whole(table.shape),
    ]
    return call(
        functools.partial(query_body, rows, tail, part),
        scal,
        ins,
        specs,
        (struct((total, cols), BF), struct((total, width), BF), struct((total, width), BF)),
        (
            pl.BlockSpec((total, tile), lambda i, sc: (0, i)),
            whole((total, width)),
            whole((total, width)),
        ),
        (cols // tile,),
        flops=2 * total * width * cols,
        nbytes=2 * width * cols + 6 * total * width,
    )


def kv_body(rows, tail, seq, steps, sc, attn_in, weight, bias, table, *refs):
    keys, values = refs[:2]
    at = pl.program_id(0)
    out = jnp.dot(attn_in[...], weight[0], preferred_element_type=F32) + bias[0]
    live = lax.broadcasted_iota(jnp.int32, (rows, 1), 0) < sc[LIMITS + 2 * seq + 1]

    @pl.when(at < steps)
    def _():
        turned = turn(out, table, 0)
        keys[0] = jnp.where(live, turned[:rows], 0.0).astype(BF)
        if tail:
            refs[2][...] = turned[rows:].astype(BF)

    @pl.when(at >= steps)
    def _():
        values[0] = jnp.where(live, out[:rows], 0.0).astype(BF)
        if tail:
            refs[3][...] = out[rows:].astype(BF)


def new_kv(scal, seq, rows, attn_in, weight, bias, table):
    total, width = attn_in.shape
    tail = total - rows
    cols = weight.shape[2]
    tile = min(256, cols)
    steps = cols // tile
    ins = [attn_in, weight, bias, table]
    specs = [
        whole(attn_in.shape),
        pl.BlockSpec((1, width, tile), lambda i, sc: (1 + i // steps, 0, i % steps)),
        pl.BlockSpec((1, 1, tile), lambda i, sc: (1 + i // steps, 0, i % steps)),
        whole(table.shape),
    ]
    outs = [struct((1, rows, cols), BF)] * 2
    key_at = lambda i, sc: (0, 0, jnp.minimum(i, steps - 1))
    value_at = lambda i, sc: (0, 0, jnp.maximum(i - steps, 0))
    out_specs = [pl.BlockSpec((1, rows, tile), key_at), pl.BlockSpec((1, rows, tile), value_at)]
    if tail:
        outs += [struct((tail, cols), BF)] * 2
        out_specs += [
            pl.BlockSpec((tail, tile), lambda i, sc: (0, jnp.minimum(i, steps - 1))),
            pl.BlockSpec((tail, tile), lambda i, sc: (0, jnp.maximum(i - steps, 0))),
        ]
    return call(
        functools.partial(kv_body, rows, tail, seq, steps),
        scal,
        ins,
        specs,
        outs,
        out_specs,
        (2 * steps,),
        flops=4 * total * width * cols,
        nbytes=4 * width * cols + 2 * total * width,
    )


def attend(query, pieces):
    scores = []
    for keys, _, limit in pieces:
        s = lax.dot_general(
            query, keys, (((1,), (1,)), ((), ())), preferred_element_type=F32
        )
        col = lax.broadcasted_iota(jnp.int32, s.shape, 1)
        scores.append(jnp.where(col < limit, s, NEG))
    top = functools.reduce(
        jnp.maximum, [jnp.max(s, axis=-1, keepdims=True) for s in scores]
    )
    total = 0.0
    acc = 0.0
    for s, (_, values, _) in zip(scores, pieces, strict=True):
        weight = jnp.exp2((s - top) * (SCALE * math.log2(math.e)))
        total = total + jnp.sum(weight, axis=-1, keepdims=True)
        acc = acc + jnp.dot(weight.astype(BF), values, preferred_element_type=F32)
    return acc / total, top * SCALE + jnp.log(total)


def pack_rows(rows_of):
    index = lax.broadcasted_iota(jnp.int32, (LSE, HD), 0)
    tile = jnp.zeros((LSE, HD), F32)
    n = len(rows_of)
    for b, row in enumerate(rows_of):
        row = jnp.broadcast_to(row, (LSE, HD))
        for piece in range(3):
            short = row.astype(BF).astype(F32)
            tile = jnp.where(index == piece * n + b, short, tile)
            row = row - short
    return tile.astype(BF)


def unpack_rows(tile, n):
    tile = tile.astype(F32)
    return [tile[b : b + 1] + tile[n + b : n + b + 1] + tile[2 * n + b : 2 * n + b + 1] for b in range(n)]


def store_partial(ref, result, logsum):
    rows = result.shape[0]
    ref[pl.ds(0, rows), :] = result.astype(BF)
    packed = []
    for b in range(rows // HD):
        col = jnp.broadcast_to(logsum[b * HD : (b + 1) * HD], (HD, HD))
        packed.append(jnp.transpose(col)[0:1])
    ref[pl.ds(rows, LSE), :] = pack_rows(packed)


def own_body(rows, seq, sc, q, qdec, kc, vc, kn, vn, *refs):
    if seq > 0:
        dec_in, refs = refs[0], refs[1:]
    out, dec_out = refs
    pre, new = sc[LIMITS + 2 * seq], sc[LIMITS + 2 * seq + 1]
    row = lax.broadcasted_iota(jnp.int32, (rows, 1), 0)
    result, logsum = attend(
        q[...],
        [(kc[0], vc[0], pre), (kn[0], vn[0], jnp.minimum(row + 1, new))],
    )
    store_partial(out, result, logsum)
    result, logsum = attend(qdec[...], [(kc[0], vc[0], pre), (kn[0], vn[0], new)])
    logsum = jnp.broadcast_to(logsum, (DEC, HD))
    if seq > 0:
        mine = lax.broadcasted_iota(jnp.int32, (DEC, 1), 0) == seq
        result = jnp.where(mine, result, dec_in[pl.ds(0, DEC), :])
        logsum = jnp.where(mine, logsum, dec_in[pl.ds(DEC, DEC), :])
    dec_out[pl.ds(0, DEC), :] = result
    dec_out[pl.ds(DEC, DEC), :] = logsum


def kv_specs(seq, pre, rows):
    return [
        pl.BlockSpec((1, pre, HD), lambda h, sc: (seq, 0, h)),
        pl.BlockSpec((1, pre, HD), lambda h, sc: (seq, 0, h)),
        pl.BlockSpec((1, rows, HD), lambda h, sc: (0, 0, h)),
        pl.BlockSpec((1, rows, HD), lambda h, sc: (0, 0, h)),
    ]


def attend_own(scal, seq, rows, q, q_first, kv, dec):
    cols = q.shape[1]
    pre = kv[0].shape[1]
    block = pl.BlockSpec((rows + LSE, HD), lambda h, sc: (0, h))
    dec_block = pl.BlockSpec((2 * DEC, HD), lambda h, sc: (0, h))
    ins = [q, q_first, *kv]
    specs = [
        pl.BlockSpec((rows, HD), lambda h, sc: (0, h)),
        pl.BlockSpec((DEC, HD), lambda h, sc: (rows // DEC, h)),
        *kv_specs(seq, pre, rows),
    ]
    if seq > 0:
        ins.append(dec)
        specs.append(dec_block)
    return call(
        functools.partial(own_body, rows, seq),
        scal,
        ins,
        specs,
        (struct((rows + LSE, cols), BF), struct((2 * DEC, cols), F32)),
        (block, dec_block),
        (cols // HD,),
        flops=4 * rows * (pre + rows) * cols,
        nbytes=4 * (pre + rows) * cols,
    )


def far_body(rows, seq, step, n, sc, ql, qr, kc, vc, kn, vn, out_l, out_r):
    rank = sc[RANK]
    pre, new = sc[LIMITS + 2 * seq], sc[LIMITS + 2 * seq + 1]

    @pl.when(rank + step < n)
    def _():
        result, logsum = attend(ql[...], [(kc[0], vc[0], pre), (kn[0], vn[0], new)])
        store_partial(out_l, result, logsum)

    @pl.when(rank >= step)
    def _():
        result, logsum = attend(qr[...], [(kc[0], vc[0], pre)])
        store_partial(out_r, result, logsum)


def attend_far(scal, seq, rows, step, n, ql, qr, kv):
    cols = ql.shape[1]
    pre = kv[0].shape[1]
    block = pl.BlockSpec((rows + LSE, HD), lambda h, sc: (0, h))
    q_block = pl.BlockSpec((rows, HD), lambda h, sc: (0, h))
    return call(
        functools.partial(far_body, rows, seq, step, n),
        scal,
        [ql, qr, *kv],
        [q_block, q_block, *kv_specs(seq, pre, rows)],
        (struct((rows + LSE, cols), BF),) * 2,
        (block, block),
        (cols // HD,),
        flops=4 * rows * (pre + rows) * cols,
        nbytes=4 * (pre + rows) * cols,
    )


def blend(parts, rows):
    n = rows // HD
    logs = []
    for ref, valid in parts:
        logs.append(
            [jnp.where(valid, r, NEG) for r in unpack_rows(ref[pl.ds(rows, LSE), :], n)]
        )
    results, sums = [], []
    for b in range(n):
        row = [log[b] for log in logs]
        top = functools.reduce(jnp.maximum, row)
        weights = [jnp.exp(r - top) for r in row]
        total = functools.reduce(lambda x, y: x + y, weights)
        sums.append(top + jnp.log(total))
        acc = 0.0
        for (ref, valid), w in zip(parts, weights, strict=True):
            share = jnp.transpose(jnp.broadcast_to(w / total, (HD, HD)))
            acc = acc + share * ref[pl.ds(b * HD, HD), :].astype(F32)
        results.append(acc)
    return results, sums


def merge_body(rows, step, n, sc, mine_l, got_l, mine_r, got_r, out_l, out_r):
    rank = sc[RANK]
    for mine, got, out, valid in (
        (mine_l, got_l, out_l, rank >= 1),
        (mine_r, got_r, out_r, rank <= n - 2),
    ):
        results, sums = blend([(mine, True), (got, valid)], rows)
        for b, r in enumerate(results):
            out[pl.ds(b * HD, HD), :] = r.astype(BF)
        out[pl.ds(rows, LSE), :] = pack_rows(sums)


def merge(scal, rows, step, n, mine_l, got_l, mine_r, got_r):
    total, cols = mine_l.shape
    block = pl.BlockSpec((total, HD), lambda h, sc: (0, h))
    return call(
        functools.partial(merge_body, rows, step, n),
        scal,
        [mine_l, got_l, mine_r, got_r],
        [block] * 4,
        (struct((total, cols), BF),) * 2,
        (block, block),
        (cols // HD,),
        nbytes=12 * total * cols,
    )


def decode_body(n, sc, q, k, v, *refs):
    parts, out = refs[:n], refs[n]
    own = jnp.sum(q[...].astype(F32) * k[...].astype(F32), axis=-1, keepdims=True) * SCALE
    own = jnp.broadcast_to(own, (DEC, HD))
    logs = [p[pl.ds(DEC, DEC), :] for p in parts]
    top = functools.reduce(jnp.maximum, logs, own)
    share = jnp.exp(own - top)
    total = share
    acc = share.astype(BF).astype(F32) * v[...].astype(F32)
    for p, log in zip(parts, logs, strict=True):
        share = jnp.exp(log - top)
        total = total + share
        acc = acc + share * p[pl.ds(0, DEC), :]
    out[...] = (acc / total).astype(BF)


def decode_attn(scal, rows, q_first, k_dec, v_dec, parts):
    cols = q_first.shape[1]
    block = pl.BlockSpec((DEC, HD), lambda h, sc: (0, h))
    return call(
        functools.partial(decode_body, len(parts)),
        scal,
        [q_first, k_dec, v_dec, *parts],
        [pl.BlockSpec((DEC, HD), lambda h, sc: (rows // DEC, h)), block, block]
        + [pl.BlockSpec((2 * DEC, HD), lambda h, sc: (0, h))] * len(parts),
        struct((DEC, cols), BF),
        block,
        (cols // HD,),
    )


def up_body(count, sc, *refs):
    weight, bias = refs[count : count + 2]
    for x, out in zip(refs[:count], refs[count + 2 :], strict=True):
        y = jnp.dot(x[...], weight[...], preferred_element_type=F32) + bias[...]
        out[...] = (0.5 * y * (1.0 + lax.erf(y * math.sqrt(0.5)))).astype(BF)


def up_proj(scal, xs, weight, bias):
    width, units = weight.shape
    tile = 256
    total = sum(x.shape[0] for x in xs)
    return call(
        functools.partial(up_body, len(xs)),
        scal,
        [*xs, weight, bias],
        [whole(x.shape) for x in xs]
        + [
            pl.BlockSpec((width, tile), lambda i, sc: (0, i)),
            pl.BlockSpec((1, tile), lambda i, sc: (0, i)),
        ],
        tuple(struct((x.shape[0], units), BF) for x in xs),
        tuple(pl.BlockSpec((x.shape[0], tile), lambda i, sc: (0, i)) for x in xs),
        (units // tile,),
        flops=2 * total * width * units,
        nbytes=2 * width * units + 2 * total * width,
    )


def target(i):
    return jnp.where(i < 4, 7 - 2 * i, 14 - 2 * i)


def down_body(count, sc, *refs):
    weight = refs[count]
    for x, out in zip(refs[:count], refs[count + 1 :], strict=True):
        out[0] = jnp.dot(x[...], weight[...], preferred_element_type=F32)


def down_proj(scal, xs, weight, part):
    units, width = weight.shape
    total = sum(x.shape[0] for x in xs)
    return call(
        functools.partial(down_body, len(xs)),
        scal,
        [*xs, weight],
        [whole(x.shape) for x in xs]
        + [pl.BlockSpec((units, part), lambda i, sc: (0, sc[ME] ^ target(i)))],
        tuple(struct((8, x.shape[0], part), F32) for x in xs),
        tuple(pl.BlockSpec((1, x.shape[0], part), lambda i, sc: (i, 0, 0)) for x in xs),
        (8,),
        flops=2 * total * width * units,
        nbytes=2 * width * units + 4 * total * width,
    )


def out_body(rows, tail, n, sc, mine, got_l, got_r, *refs):
    if tail:
        dec, refs = refs[0], refs[1:]
    weight, mlp, odd, even, attn = refs
    rank = sc[RANK]
    i = pl.program_id(0)

    @pl.when(i == 0)
    def _():
        for h in range(mine.shape[1] // HD):
            at = slice(h * HD, (h + 1) * HD)
            parts = [
                (mine.at[:, at], True),
                (got_l.at[:, at], rank >= 1),
                (got_r.at[:, at], rank <= n - 2),
            ]
            results, _ = blend(parts, rows)
            for b, r in enumerate(results):
                attn[pl.ds(b * HD, HD), at] = r.astype(BF)
        if tail:
            attn[pl.ds(rows, tail), :] = dec[...]

    out = (jnp.dot(attn[...], weight[...], preferred_element_type=F32) + mlp[0]).astype(BF)

    @pl.when(i < 4)
    def _():
        odd[0] = out

    @pl.when(i >= 4)
    def _():
        even[0] = out


def out_proj(scal, rows, n, mine, got_l, got_r, dec, weight, mlp):
    cols, width = weight.shape
    part = mlp.shape[2]
    total = mlp.shape[1]
    tail = total - rows
    ins = [mine, got_l, got_r] + ([dec] if tail else []) + [weight, mlp]
    specs = [whole(a.shape) for a in ins[:-2]] + [
        pl.BlockSpec((cols, part), lambda i, sc: (0, sc[ME] ^ target(i))),
        pl.BlockSpec((1, total, part), lambda i, sc: (i, 0, 0)),
    ]
    return call(
        functools.partial(out_body, rows, tail, n),
        scal,
        ins,
        specs,
        (struct((4, total, part), BF),) * 2,
        (
            pl.BlockSpec((1, total, part), lambda i, sc: (jnp.minimum(i, 3), 0, 0)),
            pl.BlockSpec((1, total, part), lambda i, sc: (jnp.maximum(i - 4, 0), 0, 0)),
        ),
        (8,),
        scratch=[pltpu.VMEM((total, cols), BF)],
        flops=2 * total * width * cols,
        nbytes=2 * width * cols + 6 * total * width,
    )


def swap(value, bit):
    return hop(value, "tp", [(i, i ^ bit) for i in range(8)])


def gather_rows(own):
    half = own.shape[0] // 2
    x, y, c = swap(own, 2), swap(own, 4), swap(own, 1)
    da, db = swap(y[:half], 2), swap(x[half:], 4)
    cx, cy = swap(x, 1), swap(y, 1)
    ca, cb = swap(da, 1), swap(db, 1)
    return [own, c, x, cx, y, cy, da, db, ca, cb]


def scatter_rows(odd, even, rows):
    half = rows // 2

    def both(a, b):
        return a.astype(F32) + b.astype(F32)

    other = swap(odd, 1)
    far = both(even[0], other[0]).astype(BF)
    got_y, got_x = swap(far[:half], 2), swap(far[half:], 4)
    to_y = both(even[1], other[1])
    to_y = jnp.concatenate([to_y[:half] + got_y.astype(F32), to_y[half:]], axis=0).astype(BF)
    to_x = both(even[2], other[2])
    to_x = jnp.concatenate([to_x[:half], to_x[half:] + got_x.astype(F32)], axis=0).astype(BF)
    from_x, from_y = swap(to_x, 2), swap(to_y, 4)
    return both(even[3], other[3]) + both(from_x, from_y)


def rope_table(position):
    lane = jnp.arange(HD, dtype=jnp.int32)
    half = ROT // 2
    freqs = jnp.exp((lane % half).astype(F32) * (-2.0 * math.log(10000.0) / ROT))
    angle = position.astype(F32)[:, None] * freqs[None, :]
    cosine = jnp.where(lane < ROT, jnp.cos(angle), 1.0)
    sine = jnp.sin(angle)
    down = jnp.where(lane < half, -sine, 0.0)
    up = jnp.where((lane >= half) & (lane < ROT), sine, 0.0)
    return jnp.stack([cosine, down, up])


def moved_queries(
    hidden_in,
    decode_in,
    pre_len,
    new_len,
    key_cache,
    value_cache,
    ln_attn_gain,
    ln_attn_bias,
    ln_mlp_gain,
    ln_mlp_bias,
    qkv_weight,
    qkv_bias,
    out_weight,
    out_bias,
    up_weight,
    up_bias,
    down_weight,
    down_bias,
):
    seqs, rows, part = hidden_in.shape
    pre = key_cache.shape[1]
    n = lax.axis_size("ctx")
    rank = lax.axis_index("ctx")
    me = lax.axis_index("tp")
    right = [(i, i + 1) for i in range(n - 1)]
    left = [(i + 1, i) for i in range(n - 1)]
    pre_here = jnp.clip(pre_len - rank * pre, 0, pre)
    new_here = jnp.clip(new_len - rank * rows, 0, rows)
    limits = jnp.stack([pre_here, new_here], axis=1).reshape(-1)
    scal = jnp.concatenate([jnp.stack([me, rank]), limits]).astype(jnp.int32)
    norms = jnp.stack([ln_attn_gain, ln_attn_bias, ln_mlp_gain, ln_mlp_bias])
    bias3 = qkv_bias[:, None, :]
    dec_rows = jnp.pad(decode_in, ((0, DEC - seqs), (0, 0)))
    index = rank * rows + jnp.arange(rows, dtype=jnp.int32)
    dec_pos = jnp.pad(pre_len + new_len, (0, DEC - seqs))

    q, mlp_in, near = [], [], []
    tables, attn_ins = [], []
    for s in range(seqs):
        position = pre_len[s] + index
        if s == 0:
            position = jnp.concatenate([position, dec_pos])
        tables.append(rope_table(position))
        blocks = gather_rows(hidden_in[s])
        qs, attn_in, mlp = queries(
            scal, blocks, dec_rows if s == 0 else None, norms, qkv_weight, bias3, tables[s]
        )
        q.append(qs)
        mlp_in.append(mlp)
        attn_ins.append(attn_in)

    def spread(s):
        toward_l, toward_r = [], []
        here = q[s][:rows]
        l, r = here, here
        for step in range(1, n):
            l = hop(l, "ctx", left[: n - step])
            r = hop(r, "ctx", right[step - 1 :])
            toward_l.append(l)
            toward_r.append(r)
        return toward_l, toward_r

    far_q = [spread(s) for s in range(seqs)]
    for s in range(seqs):
        got = new_kv(scal, s, rows, attn_ins[s], qkv_weight, bias3, tables[s])
        if s == 0:
            k_dec, v_dec = got[2:]
        near.append(got[:2])
    new_keys, new_values = (
        jnp.concatenate([pair[i] for pair in near], axis=0) for i in range(2)
    )

    dec = None
    own_out, far_out = [], []
    for s in range(seqs):
        kv = (key_cache, value_cache, *near[s])
        result, dec = attend_own(scal, s, rows, q[s], q[0], kv, dec)
        own_out.append(result)
        far_out.append(
            [
                attend_far(scal, s, rows, step, n, far_q[s][0][step - 1], far_q[s][1][step - 1], kv)
                for step in range(1, n)
            ]
        )
    dec_parts = [dec] + [
        hop(dec, "ctx", [(i, (i + k) % n) for i in range(n)]) for k in range(1, n)
    ]
    attn_dec = decode_attn(scal, rows, q[0], k_dec, v_dec, dec_parts)

    ups = up_proj(scal, mlp_in, up_weight, up_bias[None, :])
    mlps = down_proj(scal, ups, down_weight, part)

    bias = lax.dynamic_slice_in_dim(out_bias + down_bias, me * part, part)
    prefill = []
    for s in range(seqs):
        mine_l, mine_r = far_out[s][n - 2]
        for step in range(n - 1, 0, -1):
            got_l = hop(mine_l, "ctx", right[: n - step])
            got_r = hop(mine_r, "ctx", left[step - 1 :])
            if step > 1:
                next_l, next_r = far_out[s][step - 2]
                mine_l, mine_r = merge(scal, rows, step - 1, n, next_l, got_l, next_r, got_r)
        odd, even = out_proj(
            scal, rows, n, own_out[s], got_l, got_r, attn_dec if s == 0 else None, out_weight, mlps[s]
        )
        summed = scatter_rows(odd, even, rows)
        live = index < new_len[s]
        full = hidden_in[s].astype(F32) + summed[:rows] + bias
        prefill.append(jnp.where(live[:, None], full, 0.0).astype(BF))
        if s == 0:
            resid = lax.dynamic_slice_in_dim(decode_in, me * part, part, 1)
            decode_out = (resid.astype(F32) + summed[rows : rows + seqs] + bias).astype(BF)
    return (jnp.stack(prefill), new_keys, new_values, decode_out)


def layer(ctx, tp, *args):
    rows, cols = args[0].shape[1], args[10].shape[2]
    fits = tp == 8 and ctx >= 2 and rows % 256 == 0 and rows // HD * 3 <= LSE and cols % 256 == 0
    if fits and args[4].shape[1] % 128 == 0 and args[0].shape[0] <= DEC:
        return moved_queries(*args)
    return shards(*args)


def solution(mesh):
    return jax.shard_map(
        functools.partial(layer, mesh.shape["ctx"], mesh.shape["tp"]),
        mesh=mesh,
        in_specs=(
            P(None, "ctx", "tp"),
            P(),
            P(),
            P(),
            P(None, "ctx", "tp"),
            P(None, "ctx", "tp"),
            P(),
            P(),
            P(),
            P(),
            P(None, None, "tp"),
            P(None, "tp"),
            P("tp", None),
            P(),
            P(None, "tp"),
            P("tp"),
            P("tp", None),
            P(),
        ),
        out_specs=(P(None, "ctx", "tp"), P(None, "ctx", "tp"), P(None, "ctx", "tp"), P(None, "tp")),
        check_vma=False,
    )
```

```python
import functools
import math

import jax
import jax.numpy as jnp
from jax import lax
from jax.experimental import pallas as pl
from jax.experimental.pallas import tpu as pltpu
from jax.sharding import PartitionSpec as P

HD = 128
ROT = 32


EPS = 1e-05
NEG = -1e30


def joined_2(part, axis, combine):
    gathered = jax.tree.map(lambda a: lax.all_gather(a, axis), part)

    def take(source):
        return jax.tree.map(lambda a: lax.dynamic_index_in_dim(a, source, 0, False), gathered)

    return lax.fori_loop(
        1, lax.axis_size(axis), lambda source, state: combine(state, take(source)), take(0)
    )


def norm_rows(rows, gain, shift):
    values = rows.astype(jnp.float32)
    center = values - jnp.mean(values, axis=-1, keepdims=True)
    spread = jnp.mean(center * center, axis=-1, keepdims=True)
    return (center * lax.rsqrt(spread + EPS) * gain + shift).astype(jnp.bfloat16)


def rotate(values, position):
    half = ROT // 2
    freqs = jnp.exp(jnp.arange(half, dtype=jnp.float32) * (-2.0 * math.log(10000.0) / ROT))
    angle = position.astype(jnp.float32)[..., None] * freqs
    cosine = jnp.cos(angle)
    sine = jnp.sin(angle)
    first = values[..., :half]
    second = values[..., half:ROT]
    return jnp.concatenate(
        [first * cosine - second * sine, second * cosine + first * sine, values[..., ROT:]], axis=-1
    )


def key_status(first, count, pre_dev, new_dev, pre_len, new_len):
    index = first + jnp.arange(count, dtype=jnp.int32)
    owner = index // (pre_dev + new_dev)
    offset = index % (pre_dev + new_dev)
    is_prefix = offset < pre_dev
    prefix_pos = owner * pre_dev + offset
    new_pos = owner * new_dev + offset - pre_dev
    prefix_ok = is_prefix[None, :] & (prefix_pos[None, :] < pre_len[:, None])
    new_ok = jnp.logical_not(is_prefix)[None, :] & (new_pos[None, :] < new_len[:, None])
    return (prefix_ok, new_ok, new_pos)


def absorb(state, queries, keys, values, allowed):
    top, total, acc = state
    scores = jnp.einsum("sqhd,skhd->shqk", queries, keys, preferred_element_type=jnp.float32) * (
        1.0 / math.sqrt(HD)
    )
    mask = allowed[:, None]
    scores = jnp.where(mask, scores, NEG)
    new_top = jnp.maximum(top, jnp.max(scores, axis=-1))
    weight = jnp.where(mask, jnp.exp(scores - new_top[..., None]), 0.0)
    factor = jnp.exp(top - new_top)
    total = total * factor + jnp.sum(weight, axis=-1)
    acc = acc * factor[..., None] + jnp.einsum(
        "shqk,skhd->shqd", weight.astype(jnp.bfloat16), values, preferred_element_type=jnp.float32
    )
    return (new_top, total, acc)


def empty_state(seqs, heads_dev, count):
    return (
        jnp.full((seqs, heads_dev, count), NEG, jnp.float32),
        jnp.zeros((seqs, heads_dev, count), jnp.float32),
        jnp.zeros((seqs, heads_dev, count, HD), jnp.float32),
    )


def join_parts(first, second):
    best = jnp.maximum(first[0], second[0])
    left = jnp.exp(first[0] - best)
    right = jnp.exp(second[0] - best)
    return (
        best,
        first[1] * left + second[1] * right,
        first[2] * left[..., None] + second[2] * right[..., None],
    )


def shards(
    hidden_in,
    decode_in,
    pre_len,
    new_len,
    key_cache,
    value_cache,
    ln_attn_gain,
    ln_attn_bias,
    ln_mlp_gain,
    ln_mlp_bias,
    qkv_weight,
    qkv_bias,
    out_weight,
    out_bias,
    up_weight,
    up_bias,
    down_weight,
    down_bias,
):
    seqs, new_dev, part_cols = hidden_in.shape
    pre_dev = key_cache.shape[1]
    local_cols = qkv_weight.shape[2]
    heads_dev = local_cols // HD
    width = decode_in.shape[1]
    block_len = pre_dev + new_dev
    rows_new = seqs * new_dev
    ctx_rank = lax.axis_index("ctx")
    tp_rank = lax.axis_index("tp")
    whole = lax.all_gather(hidden_in, "tp", axis=2, tiled=True)
    joined = jnp.concatenate([whole.reshape(rows_new, width), decode_in], axis=0)
    attn_in = norm_rows(joined, ln_attn_gain, ln_attn_bias)
    mlp_in = norm_rows(joined, ln_mlp_gain, ln_mlp_bias)
    proj = [
        jnp.dot(attn_in, qkv_weight[i], preferred_element_type=jnp.float32) + qkv_bias[i]
        for i in range(3)
    ]
    up_act = jax.nn.gelu(
        jnp.dot(mlp_in, up_weight, preferred_element_type=jnp.float32) + up_bias, approximate=False
    ).astype(jnp.bfloat16)
    query_index = ctx_rank * new_dev + jnp.arange(new_dev, dtype=jnp.int32)
    position = pre_len[:, None] + query_index[None, :]
    dec_position = pre_len + new_len
    q_new = rotate(
        proj[0][:rows_new].reshape(seqs, new_dev, heads_dev, HD), position[..., None]
    ).astype(jnp.bfloat16)
    k_new = rotate(
        proj[1][:rows_new].reshape(seqs, new_dev, heads_dev, HD), position[..., None]
    ).astype(jnp.bfloat16)
    v_new = proj[2][:rows_new].reshape(seqs, new_dev, heads_dev, HD).astype(jnp.bfloat16)
    q_dec = rotate(proj[0][rows_new:].reshape(seqs, heads_dev, HD), dec_position[:, None]).astype(
        jnp.bfloat16
    )
    k_dec = rotate(proj[1][rows_new:].reshape(seqs, heads_dev, HD), dec_position[:, None]).astype(
        jnp.bfloat16
    )
    v_dec = proj[2][rows_new:].reshape(seqs, heads_dev, HD).astype(jnp.bfloat16)
    live = query_index[None, :] < new_len[:, None]
    flat_keys = k_new.reshape(seqs, new_dev, local_cols)
    flat_values = v_new.reshape(seqs, new_dev, local_cols)
    new_keys = jnp.where(live[..., None], flat_keys, 0)
    new_values = jnp.where(live[..., None], flat_values, 0)
    local_block = jnp.concatenate(
        [jnp.stack([key_cache, value_cache], axis=2), jnp.stack([flat_keys, flat_values], axis=2)],
        axis=1,
    )
    local_keys = local_block[:, :, 0].reshape(seqs, block_len, heads_dev, HD)
    local_values = local_block[:, :, 1].reshape(seqs, block_len, heads_dev, HD)

    def allowed_for(first, count, queries_at):
        prefix_ok, new_ok, new_pos = key_status(first, count, pre_dev, new_dev, pre_len, new_len)
        return prefix_ok[:, None, :] | new_ok[:, None, :] & (
            new_pos[None, None, :] <= queries_at[None, :, None]
        )

    state = empty_state(seqs, heads_dev, new_dev)
    piece = lax.all_gather(local_block, "ctx", axis=1, tiled=True)
    blocks = piece.shape[1] // block_len

    def one_block(inner, number):
        begin = number * block_len
        slab = lax.dynamic_slice_in_dim(piece, begin, block_len, 1)
        keys = slab[:, :, 0].reshape(seqs, block_len, heads_dev, HD)
        values = slab[:, :, 1].reshape(seqs, block_len, heads_dev, HD)
        allowed = allowed_for(begin, block_len, query_index)
        return (absorb(inner, q_new, keys, values, allowed), None)

    state, _ = lax.scan(one_block, state, jnp.arange(blocks, dtype=jnp.int32))
    top, total, acc = state
    attn_new = (
        (acc / total[..., None])
        .transpose(0, 2, 1, 3)
        .reshape(rows_new, local_cols)
        .astype(jnp.bfloat16)
    )
    prefix_ok, new_ok, new_pos = key_status(
        ctx_rank * block_len, block_len, pre_dev, new_dev, pre_len, new_len
    )
    dec_allowed = (prefix_ok | new_ok)[:, None, :]
    dec_state = absorb(
        empty_state(seqs, heads_dev, 1), q_dec[:, None], local_keys, local_values, dec_allowed
    )
    dec_top, dec_total, dec_acc = joined_2(dec_state, "ctx", join_parts)
    dec_top = dec_top[..., 0]
    dec_total = dec_total[..., 0]
    dec_acc = dec_acc[:, :, 0]
    own = jnp.einsum("shd,shd->sh", q_dec, k_dec, preferred_element_type=jnp.float32) * (
        1.0 / math.sqrt(HD)
    )
    best = jnp.maximum(dec_top, own)
    far_factor = jnp.exp(dec_top - best)
    own_weight = jnp.exp(own - best)
    dec_total = dec_total * far_factor + own_weight
    dec_acc = dec_acc * far_factor[..., None] + jnp.einsum(
        "sh,shd->shd", own_weight.astype(jnp.bfloat16), v_dec, preferred_element_type=jnp.float32
    )
    attn_dec = (dec_acc / dec_total[..., None]).reshape(seqs, local_cols).astype(jnp.bfloat16)
    attn_rows = jnp.concatenate([attn_new, attn_dec], axis=0)
    branches = jnp.dot(attn_rows, out_weight, preferred_element_type=jnp.float32) + jnp.dot(
        up_act, down_weight, preferred_element_type=jnp.float32
    )
    summed_new, summed_dec = (
        lax.psum_scatter(
            branches[:rows_new].reshape(seqs, new_dev, width).astype(jnp.bfloat16),
            "tp",
            scatter_dimension=2,
            tiled=True,
        ).astype(jnp.float32),
        lax.psum_scatter(
            branches[rows_new:].astype(jnp.bfloat16), "tp", scatter_dimension=1, tiled=True
        ).astype(jnp.float32),
    )
    bias = lax.dynamic_slice_in_dim(out_bias + down_bias, tp_rank * part_cols, part_cols)
    prefill = hidden_in.astype(jnp.float32) + summed_new + bias
    prefill_out = jnp.where(live[..., None], prefill, 0.0).astype(jnp.bfloat16)
    dec_resid = lax.dynamic_slice_in_dim(decode_in, tp_rank * part_cols, part_cols, 1)
    decode_out = (dec_resid.astype(jnp.float32) + summed_dec + bias).astype(jnp.bfloat16)
    return (prefill_out, new_keys, new_values, decode_out)


BF = jnp.bfloat16
F32 = jnp.float32
DEC = 16
LSE = 16
SCALE = 1.0 / math.sqrt(HD)


def hop(value, axis, pairs):
    return lax.ppermute(value, axis, pairs)


def call(body, scal, ins, outs, scratch=(), flops=0, nbytes=0, limit=16):
    return pl.pallas_call(
        body,
        out_shape=outs,
        in_specs=[pl.BlockSpec(memory_space=pltpu.SMEM)]
        + [pl.BlockSpec(memory_space=pltpu.VMEM)] * len(ins),
        out_specs=jax.tree.map(lambda _: pl.BlockSpec(memory_space=pltpu.VMEM), outs),
        scratch_shapes=list(scratch),
        compiler_params=pltpu.CompilerParams(vmem_limit_bytes=limit << 20),
        cost_estimate=pl.CostEstimate(flops=flops, transcendentals=0, bytes_accessed=nbytes),
    )(scal, *ins)


def struct(shape, dtype):
    return jax.ShapeDtypeStruct(tuple(shape), dtype)


ME, RANK, LIMITS = 0, 1, 2


def turn(values, table):
    cosine, down, up = (table[i] for i in range(3))
    parts = []
    for h in range(values.shape[1] // HD):
        one = values[:, h * HD : (h + 1) * HD]
        parts.append(
            one * cosine
            + pltpu.roll(one, HD - ROT // 2, 1) * down
            + pltpu.roll(one, ROT // 2, 1) * up
        )
    return jnp.concatenate(parts, axis=1)


def query_body(rows, tail, part, sc, *refs):
    blocks = refs[:10]
    refs = refs[10:]
    dec = None
    if tail:
        dec, refs = refs[0], refs[1:]
    norms, weight, bias, table, q_out, attn_in, mlp_in = refs
    me = sc[ME]
    half = rows // 2
    width = part * 8

    def finish(values, base, count, cols):
        total = functools.reduce(lambda a, b: a + b, values)
        mean = jnp.sum(total, axis=-1, keepdims=True) * (1.0 / width)
        values = [v - mean for v in values]
        square = functools.reduce(lambda a, b: a + b, [v * v for v in values])
        spread = jnp.sum(square, axis=-1, keepdims=True) * (1.0 / width)
        inv = lax.rsqrt(spread + EPS)
        for v, col in zip(values, cols, strict=True):
            v = v * inv
            at = pl.ds(col, part)
            attn_in[pl.ds(base, count), at] = (
                v * norms[pl.ds(0, 1), at] + norms[pl.ds(1, 1), at]
            ).astype(BF)
            mlp_in[pl.ds(base, count), at] = (
                v * norms[pl.ds(2, 1), at] + norms[pl.ds(3, 1), at]
            ).astype(BF)

    cols = [pl.multiple_of((me ^ k) * part, part) for k in range(8)]
    for side in range(2):
        sources = [(blocks[k], side * half) for k in range(6)]
        sources += [(blocks[6 + side], 0), (blocks[8 + side], 0)]

        def step(i, carry):
            at = pl.multiple_of(i * 16, 16)
            values = [ref[pl.ds(off + at, 16), :].astype(F32) for ref, off in sources]
            finish(values, pl.multiple_of(side * half + at, 16), 16, cols)
            return carry

        lax.fori_loop(0, half // 16, step, 0, unroll=4)
    if tail:
        values = [dec[:, pl.ds(k * part, part)].astype(F32) for k in range(8)]
        finish(values, rows, tail, [k * part for k in range(8)])
    out = jnp.dot(attn_in[...], weight[...], preferred_element_type=F32) + bias[pl.ds(0, 1), :]
    q_out[...] = turn(out, table).astype(BF)


def queries(scal, blocks, dec, norms, weight, bias, table):
    rows, part = blocks[0].shape
    tail = 0 if dec is None else DEC
    width, cols = weight.shape
    total = rows + tail
    return call(
        functools.partial(query_body, rows, tail, part),
        scal,
        [*blocks] + ([dec] if tail else []) + [norms, weight, bias, table],
        (struct((total, cols), BF), struct((total, width), BF), struct((total, width), BF)),
        flops=2 * total * width * cols,
        nbytes=2 * width * cols + 6 * total * width,
    )


def kv_body(rows, tail, seq, sc, attn_in, wk, wv, bias, table, keys, values, values_t, *dec):
    live = lax.broadcasted_iota(jnp.int32, (rows, 1), 0) < sc[LIMITS + 2 * seq + 1]
    out = jnp.dot(attn_in[...], wk[...], preferred_element_type=F32) + bias[pl.ds(1, 1), :]
    out = turn(out, table)
    keys[...] = jnp.where(live, out[:rows], 0.0).astype(BF)
    if tail:
        dec[0][...] = out[rows:].astype(BF)
    out = jnp.dot(attn_in[...], wv[...], preferred_element_type=F32) + bias[pl.ds(2, 1), :]
    value = jnp.where(live, out[:rows], 0.0)
    values[...] = value.astype(BF)
    values_t[...] = jnp.transpose(value).astype(BF)
    if tail:
        dec[1][...] = out[rows:].astype(BF)


def new_kv(scal, seq, rows, attn_in, wk, wv, bias, table):
    total, width = attn_in.shape
    tail = total - rows
    cols = wk.shape[1]
    outs = [struct((rows, cols), BF)] * 2 + [struct((cols, rows), BF)]
    if tail:
        outs += [struct((tail, cols), BF)] * 2
    return call(
        functools.partial(kv_body, rows, tail, seq),
        scal,
        [attn_in, wk, wv, bias, table],
        tuple(outs),
        flops=4 * total * width * cols,
        nbytes=4 * width * cols + 2 * total * width,
    )


def attend(query, pieces):
    scores = []
    for keys, _, limit in pieces:
        s = lax.dot_general(query, keys, (((1,), (1,)), ((), ())), preferred_element_type=F32)
        col = lax.broadcasted_iota(jnp.int32, s.shape, 1)
        scores.append(jnp.where(col < limit, s, NEG))
    top = functools.reduce(jnp.maximum, [jnp.max(s, axis=-1, keepdims=True) for s in scores])
    total = 0.0
    acc = 0.0
    for s, (_, values_t, _) in zip(scores, pieces, strict=True):
        weight = jnp.exp2((s - top) * (SCALE * math.log2(math.e)))
        total = total + jnp.sum(weight, axis=-1, keepdims=True)
        acc = acc + lax.dot_general(
            weight.astype(BF), values_t, (((1,), (1,)), ((), ())), preferred_element_type=F32
        )
    return acc / total, top * SCALE + jnp.log(total)


def attend_t(query, pieces):
    scores = []
    for keys, _, limit in pieces:
        s = lax.dot_general(keys, query, (((1,), (1,)), ((), ())), preferred_element_type=F32)
        row = lax.broadcasted_iota(jnp.int32, s.shape, 0)
        scores.append(jnp.where(row < limit, s, NEG))
    top = functools.reduce(jnp.maximum, [jnp.max(s, axis=0, keepdims=True) for s in scores])
    total = 0.0
    acc = 0.0
    for s, (_, values_t, _) in zip(scores, pieces, strict=True):
        weight = jnp.exp2((s - top) * (SCALE * math.log2(math.e)))
        total = total + jnp.sum(weight, axis=0, keepdims=True)
        acc = acc + jnp.dot(values_t, weight.astype(BF), preferred_element_type=F32)
    return acc / total, top * SCALE + jnp.log(total)


def pack_logs(logs):
    logs = jnp.concatenate(logs, axis=0)
    pieces = []
    for _ in range(3):
        short = logs.astype(BF).astype(F32)
        pieces.append(short)
        logs = logs - short
    return jnp.concatenate(pieces + [jnp.zeros_like(logs)], axis=0).astype(BF)


def unpack_logs(tile):
    tile = tile.astype(F32)
    return (tile[0:4] + tile[4:8]) + tile[8:12]


def head_slices(cols):
    return [slice(h * HD, (h + 1) * HD) for h in range(cols // HD)]


def attend_all(q, kc, vc, kn, vn, pre, new, out, rows):
    logs = []
    for at in head_slices(q.shape[1]):
        pieces = [(kc[:, at], vc[at, :], pre)]
        if kn is not None:
            pieces.append((kn[:, at], vn[at, :], new))
        result, log = attend_t(q[pl.ds(0, rows), at], pieces)
        out[at, :] = result.astype(BF)
        logs.append(log)
    out[pl.ds(q.shape[1], LSE), :] = pack_logs(logs)


def own_body(rows, seq, sc, q, qdec, kc, vc, kn, vn, *refs):
    if seq > 0:
        dec_in, refs = refs[0], refs[1:]
    out, dec_out = refs
    pre, new = sc[LIMITS + 2 * seq], sc[LIMITS + 2 * seq + 1]
    kc, vc = kc.at[seq], vc.at[seq]
    col = lax.broadcasted_iota(jnp.int32, (1, rows), 1)
    attend_all(q, kc, vc, kn, vn, pre, jnp.minimum(col + 1, new), out, rows)
    mine = lax.broadcasted_iota(jnp.int32, (DEC, 1), 0) == seq
    for at in head_slices(q.shape[1]):
        result, log = attend(
            qdec[pl.ds(rows, DEC), at], [(kc[:, at], vc[at, :], pre), (kn[:, at], vn[at, :], new)]
        )
        log = jnp.broadcast_to(log, (DEC, HD))
        if seq > 0:
            result = jnp.where(mine, result, dec_in[pl.ds(0, DEC), at])
            log = jnp.where(mine, log, dec_in[pl.ds(DEC, DEC), at])
        dec_out[pl.ds(0, DEC), at] = result
        dec_out[pl.ds(DEC, DEC), at] = log


def attend_own(scal, seq, rows, q, q_first, kv, dec):
    cols = q.shape[1]
    pre = kv[0].shape[1]
    return call(
        functools.partial(own_body, rows, seq),
        scal,
        [q, q_first, *kv] + ([dec] if seq > 0 else []),
        (struct((cols + LSE, rows), BF), struct((2 * DEC, cols), F32)),
        flops=4 * rows * (pre + rows) * cols,
        nbytes=4 * (pre + rows) * cols,
    )


def far_body(rows, seq, step, n, sc, ql, qr, kc, vc, kn, vn, out_l, out_r):
    rank = sc[RANK]
    pre, new = sc[LIMITS + 2 * seq], sc[LIMITS + 2 * seq + 1]
    kc, vc = kc.at[seq], vc.at[seq]

    @pl.when(rank + step < n)
    def _():
        attend_all(ql, kc, vc, kn, vn, pre, new, out_l, rows)

    @pl.when(rank >= step)
    def _():
        attend_all(qr, kc, vc, None, None, pre, None, out_r, rows)


def attend_far(scal, seq, rows, step, n, ql, qr, kv):
    cols = ql.shape[1]
    pre = kv[0].shape[1]
    return call(
        functools.partial(far_body, rows, seq, step, n),
        scal,
        [ql, qr, *kv],
        (struct((cols + LSE, rows), BF),) * 2,
        flops=4 * rows * (pre + rows) * cols,
        nbytes=4 * (pre + rows) * cols,
    )


def blend(parts):
    cols = parts[0][0].shape[0] - LSE
    logs = [
        jnp.where(valid, unpack_logs(ref[pl.ds(cols, LSE), :]), NEG) for ref, valid in parts
    ]
    top = functools.reduce(jnp.maximum, logs)
    weights = [jnp.exp(log - top) for log in logs]
    total = functools.reduce(lambda x, y: x + y, weights)
    heads = []
    for h, at in enumerate(head_slices(cols)):
        acc = 0.0
        for w, (ref, _) in zip(weights, parts, strict=True):
            acc = acc + (w / total)[h : h + 1] * ref[at, :].astype(F32)
        heads.append(acc)
    return heads, top + jnp.log(total)


def merge_body(rows, step, n, sc, mine_l, got_l, mine_r, got_r, out_l, out_r):
    rank = sc[RANK]
    for mine, got, out, valid in (
        (mine_l, got_l, out_l, rank >= 1),
        (mine_r, got_r, out_r, rank <= n - 2),
    ):
        heads, logs = blend([(mine, True), (got, valid)])
        cols = out.shape[0] - LSE
        for at, head in zip(head_slices(cols), heads, strict=True):
            out[at, :] = head.astype(BF)
        out[pl.ds(cols, LSE), :] = pack_logs([logs])


def merge(scal, rows, step, n, mine_l, got_l, mine_r, got_r):
    total, cols = mine_l.shape
    return call(
        functools.partial(merge_body, rows, step, n),
        scal,
        [mine_l, got_l, mine_r, got_r],
        (struct((total, cols), BF),) * 2,
        nbytes=12 * total * cols,
    )


def decode_body(n, rows, sc, q, k, v, *refs):
    parts, out = refs[:n], refs[n]
    for at in head_slices(k.shape[1]):
        both = q[pl.ds(rows, DEC), at].astype(F32) * k[:, at].astype(F32)
        own = jnp.broadcast_to(jnp.sum(both, axis=-1, keepdims=True) * SCALE, (DEC, HD))
        logs = [p[pl.ds(DEC, DEC), at] for p in parts]
        top = functools.reduce(jnp.maximum, logs, own)
        share = jnp.exp(own - top)
        total = share
        acc = share.astype(BF).astype(F32) * v[:, at].astype(F32)
        for p, log in zip(parts, logs, strict=True):
            share = jnp.exp(log - top)
            total = total + share
            acc = acc + share * p[pl.ds(0, DEC), at]
        out[:, at] = (acc / total).astype(BF)


def decode_attn(scal, rows, q_first, k_dec, v_dec, parts):
    return call(
        functools.partial(decode_body, len(parts), rows),
        scal,
        [q_first, k_dec, v_dec, *parts],
        struct(k_dec.shape, BF),
    )


def up_body(count, tile, sc, *refs):
    weight, bias = refs[count : count + 2]
    xs, outs = refs[:count], refs[count + 2 :]

    def step(i, carry):
        at = pl.ds(pl.multiple_of(i * tile, tile), tile)
        for x, out in zip(xs, outs, strict=True):
            y = jnp.dot(x[...], weight[:, at], preferred_element_type=F32) + bias[:, at]
            out[:, at] = (0.5 * y * (1.0 + lax.erf(y * math.sqrt(0.5)))).astype(BF)
        return carry

    lax.fori_loop(0, weight.shape[1] // tile, step, 0)


def up_proj(scal, xs, weight, bias):
    width, units = weight.shape
    total = sum(x.shape[0] for x in xs)
    return call(
        functools.partial(up_body, len(xs), 256),
        scal,
        [*xs, weight, bias],
        tuple(struct((x.shape[0], units), BF) for x in xs),
        flops=2 * total * width * units,
        nbytes=2 * width * units + 2 * total * width,
    )


def place(k):
    return (7 - k) // 2


def down_body(count, part, sc, *refs):
    weight = refs[count]
    for x, out in zip(refs[:count], refs[count + 1 :], strict=True):
        for j in range(8):
            k = sc[ME] ^ j
            out[k] = jnp.dot(
                x[...], weight[:, j * part : (j + 1) * part], preferred_element_type=F32
            )


def down_proj(scal, xs, weight, part):
    units, width = weight.shape
    total = sum(x.shape[0] for x in xs)
    return call(
        functools.partial(down_body, len(xs), part),
        scal,
        [*xs, weight],
        tuple(struct((8, x.shape[0], part), F32) for x in xs),
        flops=2 * total * width * units,
        nbytes=2 * width * units + 4 * total * width,
    )


def out_body(rows, tail, n, part, sc, mine, got_l, got_r, *refs):
    if tail:
        dec, refs = refs[0], refs[1:]
    weight, mlp, odd, even, attn = refs
    rank = sc[RANK]
    heads, _ = blend([(mine, True), (got_l, rank >= 1), (got_r, rank <= n - 2)])
    for at, head in zip(head_slices(attn.shape[1]), heads, strict=True):
        attn[pl.ds(0, rows), at] = jnp.transpose(head).astype(BF)
    if tail:
        attn[pl.ds(rows, tail), :] = dec[...]
    for j in range(8):
        k = sc[ME] ^ j
        out = jnp.dot(
            attn[...], weight[:, j * part : (j + 1) * part], preferred_element_type=F32
        )
        out = (out + mlp[k]).astype(BF)

        @pl.when(k % 2 == 1)
        def _():
            odd[place(k)] = out

        @pl.when(k % 2 == 0)
        def _():
            even[place(k)] = out


def out_proj(scal, rows, n, mine, got_l, got_r, dec, weight, mlp):
    cols, width = weight.shape
    part = mlp.shape[2]
    total = mlp.shape[1]
    tail = total - rows
    return call(
        functools.partial(out_body, rows, tail, n, part),
        scal,
        [mine, got_l, got_r] + ([dec] if tail else []) + [weight, mlp],
        (struct((4, total, part), BF),) * 2,
        scratch=[pltpu.VMEM((total, cols), BF)],
        flops=2 * total * width * cols,
        nbytes=2 * width * cols + 6 * total * width,
    )


def swap(value, bit):
    return hop(value, "tp", [(i, i ^ bit) for i in range(8)])


def gather_rows(own):
    half = own.shape[0] // 2
    x, y, c = swap(own, 2), swap(own, 4), swap(own, 1)
    da, db = swap(y[:half], 2), swap(x[half:], 4)
    cx, cy = swap(x, 1), swap(y, 1)
    ca, cb = swap(da, 1), swap(db, 1)
    return [own, c, x, cx, y, cy, da, db, ca, cb]


def scatter_rows(odd, even, rows):
    half = rows // 2

    def both(a, b):
        return a.astype(F32) + b.astype(F32)

    other = swap(odd, 1)
    far = both(even[0], other[0]).astype(BF)
    got_y, got_x = swap(far[:half], 2), swap(far[half:], 4)
    to_y = both(even[1], other[1])
    to_y = jnp.concatenate([to_y[:half] + got_y.astype(F32), to_y[half:]], axis=0).astype(BF)
    to_x = both(even[2], other[2])
    to_x = jnp.concatenate([to_x[:half], to_x[half:] + got_x.astype(F32)], axis=0).astype(BF)
    from_x, from_y = swap(to_x, 2), swap(to_y, 4)
    return both(even[3], other[3]) + both(from_x, from_y)


def rope_table(position):
    lane = jnp.arange(HD, dtype=jnp.int32)
    half = ROT // 2
    freqs = jnp.exp((lane % half).astype(F32) * (-2.0 * math.log(10000.0) / ROT))
    angle = position.astype(F32)[:, None] * freqs[None, :]
    cosine = jnp.where(lane < ROT, jnp.cos(angle), 1.0)
    sine = jnp.sin(angle)
    down = jnp.where(lane < half, -sine, 0.0)
    up = jnp.where((lane >= half) & (lane < ROT), sine, 0.0)
    return jnp.stack([cosine, down, up])


def moved_queries(
    hidden_in,
    decode_in,
    pre_len,
    new_len,
    key_cache,
    value_cache,
    ln_attn_gain,
    ln_attn_bias,
    ln_mlp_gain,
    ln_mlp_bias,
    qkv_weight,
    qkv_bias,
    out_weight,
    out_bias,
    up_weight,
    up_bias,
    down_weight,
    down_bias,
):
    seqs, rows, part = hidden_in.shape
    pre = key_cache.shape[1]
    n = lax.axis_size("ctx")
    rank = lax.axis_index("ctx")
    me = lax.axis_index("tp")
    right = [(i, i + 1) for i in range(n - 1)]
    left = [(i + 1, i) for i in range(n - 1)]
    pre_here = jnp.clip(pre_len - rank * pre, 0, pre)
    new_here = jnp.clip(new_len - rank * rows, 0, rows)
    limits = jnp.stack([pre_here, new_here], axis=1).reshape(-1)
    scal = jnp.concatenate([jnp.stack([me, rank]), limits]).astype(jnp.int32)
    norms = jnp.stack([ln_attn_gain, ln_attn_bias, ln_mlp_gain, ln_mlp_bias])
    wq, wk, wv = (qkv_weight[i] for i in range(3))
    dec_rows = jnp.pad(decode_in, ((0, DEC - seqs), (0, 0)))
    index = rank * rows + jnp.arange(rows, dtype=jnp.int32)
    dec_pos = jnp.pad(pre_len + new_len, (0, DEC - seqs))

    values_t = jnp.swapaxes(value_cache, 1, 2)
    q, mlp_in, near = [], [], []
    tables, attn_ins = [], []
    for s in range(seqs):
        position = pre_len[s] + index
        if s == 0:
            position = jnp.concatenate([position, dec_pos])
        tables.append(rope_table(position))
        blocks = gather_rows(hidden_in[s])
        qs, attn_in, mlp = queries(
            scal, blocks, dec_rows if s == 0 else None, norms, wq, qkv_bias, tables[s]
        )
        q.append(qs)
        mlp_in.append(mlp)
        attn_ins.append(attn_in)

    def spread(s):
        toward_l, toward_r = [], []
        here = q[s][:rows]
        l, r = here, here
        for step in range(1, n):
            l = hop(l, "ctx", left[: n - step])
            r = hop(r, "ctx", right[step - 1 :])
            toward_l.append(l)
            toward_r.append(r)
        return toward_l, toward_r

    far_q = [spread(s) for s in range(seqs)]
    for s in range(seqs):
        got = new_kv(scal, s, rows, attn_ins[s], wk, wv, qkv_bias, tables[s])
        if s == 0:
            k_dec, v_dec = got[3:]
        near.append(got[:3])
    new_keys, new_values = (
        jnp.stack([pair[i] for pair in near]) for i in range(2)
    )

    dec = None
    own_out, far_out = [], []
    for s in range(seqs):
        kv = (key_cache, values_t, near[s][0], near[s][2])
        result, dec = attend_own(scal, s, rows, q[s], q[0], kv, dec)
        own_out.append(result)
        far_out.append(
            [
                attend_far(scal, s, rows, step, n, far_q[s][0][step - 1], far_q[s][1][step - 1], kv)
                for step in range(1, n)
            ]
        )
    dec_parts = [dec] + [
        hop(dec, "ctx", [(i, (i + k) % n) for i in range(n)]) for k in range(1, n)
    ]
    attn_dec = decode_attn(scal, rows, q[0], k_dec, v_dec, dec_parts)

    ups = up_proj(scal, mlp_in, up_weight, up_bias[None, :])
    mlps = down_proj(scal, ups, down_weight, part)

    bias = lax.dynamic_slice_in_dim(out_bias + down_bias, me * part, part)
    prefill = []
    for s in range(seqs):
        mine_l, mine_r = far_out[s][n - 2]
        for step in range(n - 1, 0, -1):
            got_l = hop(mine_l, "ctx", right[: n - step])
            got_r = hop(mine_r, "ctx", left[step - 1 :])
            if step > 1:
                next_l, next_r = far_out[s][step - 2]
                mine_l, mine_r = merge(scal, rows, step - 1, n, next_l, got_l, next_r, got_r)
        odd, even = out_proj(
            scal, rows, n, own_out[s], got_l, got_r, attn_dec if s == 0 else None, out_weight, mlps[s]
        )
        summed = scatter_rows(odd, even, rows)
        live = index < new_len[s]
        full = hidden_in[s].astype(F32) + summed[:rows] + bias
        prefill.append(jnp.where(live[:, None], full, 0.0).astype(BF))
        if s == 0:
            resid = lax.dynamic_slice_in_dim(decode_in, me * part, part, 1)
            decode_out = (resid.astype(F32) + summed[rows : rows + seqs] + bias).astype(BF)
    return (jnp.stack(prefill), new_keys, new_values, decode_out)


def layer(ctx, tp, *args):
    rows, cols = args[0].shape[1], args[10].shape[2]
    fits = tp == 8 and ctx >= 2 and rows % 256 == 0 and cols == 4 * HD
    if fits and args[4].shape[1] % 128 == 0 and args[0].shape[0] <= DEC:
        return moved_queries(*args)
    return shards(*args)


def solution(mesh):
    return jax.shard_map(
        functools.partial(layer, mesh.shape["ctx"], mesh.shape["tp"]),
        mesh=mesh,
        in_specs=(
            P(None, "ctx", "tp"),
            P(),
            P(),
            P(),
            P(None, "ctx", "tp"),
            P(None, "ctx", "tp"),
            P(),
            P(),
            P(),
            P(),
            P(None, None, "tp"),
            P(None, "tp"),
            P("tp", None),
            P(),
            P(None, "tp"),
            P("tp"),
            P("tp", None),
            P(),
        ),
        out_specs=(P(None, "ctx", "tp"), P(None, "ctx", "tp"), P(None, "ctx", "tp"), P(None, "tp")),
        check_vma=False,
    )
```

```python
import functools
import math

import jax
import jax.numpy as jnp
from jax import lax
from jax.experimental import pallas as pl
from jax.experimental.pallas import tpu as pltpu
from jax.sharding import PartitionSpec as P

HD = 128
ROT = 32


EPS = 1e-05
NEG = -1e30


def joined_2(part, axis, combine):
    gathered = jax.tree.map(lambda a: lax.all_gather(a, axis), part)

    def take(source):
        return jax.tree.map(lambda a: lax.dynamic_index_in_dim(a, source, 0, False), gathered)

    return lax.fori_loop(
        1, lax.axis_size(axis), lambda source, state: combine(state, take(source)), take(0)
    )


def norm_rows(rows, gain, shift):
    values = rows.astype(jnp.float32)
    center = values - jnp.mean(values, axis=-1, keepdims=True)
    spread = jnp.mean(center * center, axis=-1, keepdims=True)
    return (center * lax.rsqrt(spread + EPS) * gain + shift).astype(jnp.bfloat16)


def rotate(values, position):
    half = ROT // 2
    freqs = jnp.exp(jnp.arange(half, dtype=jnp.float32) * (-2.0 * math.log(10000.0) / ROT))
    angle = position.astype(jnp.float32)[..., None] * freqs
    cosine = jnp.cos(angle)
    sine = jnp.sin(angle)
    first = values[..., :half]
    second = values[..., half:ROT]
    return jnp.concatenate(
        [first * cosine - second * sine, second * cosine + first * sine, values[..., ROT:]], axis=-1
    )


def key_status(first, count, pre_dev, new_dev, pre_len, new_len):
    index = first + jnp.arange(count, dtype=jnp.int32)
    owner = index // (pre_dev + new_dev)
    offset = index % (pre_dev + new_dev)
    is_prefix = offset < pre_dev
    prefix_pos = owner * pre_dev + offset
    new_pos = owner * new_dev + offset - pre_dev
    prefix_ok = is_prefix[None, :] & (prefix_pos[None, :] < pre_len[:, None])
    new_ok = jnp.logical_not(is_prefix)[None, :] & (new_pos[None, :] < new_len[:, None])
    return (prefix_ok, new_ok, new_pos)


def absorb(state, queries, keys, values, allowed):
    top, total, acc = state
    scores = jnp.einsum("sqhd,skhd->shqk", queries, keys, preferred_element_type=jnp.float32) * (
        1.0 / math.sqrt(HD)
    )
    mask = allowed[:, None]
    scores = jnp.where(mask, scores, NEG)
    new_top = jnp.maximum(top, jnp.max(scores, axis=-1))
    weight = jnp.where(mask, jnp.exp(scores - new_top[..., None]), 0.0)
    factor = jnp.exp(top - new_top)
    total = total * factor + jnp.sum(weight, axis=-1)
    acc = acc * factor[..., None] + jnp.einsum(
        "shqk,skhd->shqd", weight.astype(jnp.bfloat16), values, preferred_element_type=jnp.float32
    )
    return (new_top, total, acc)


def empty_state(seqs, heads_dev, count):
    return (
        jnp.full((seqs, heads_dev, count), NEG, jnp.float32),
        jnp.zeros((seqs, heads_dev, count), jnp.float32),
        jnp.zeros((seqs, heads_dev, count, HD), jnp.float32),
    )


def join_parts(first, second):
    best = jnp.maximum(first[0], second[0])
    left = jnp.exp(first[0] - best)
    right = jnp.exp(second[0] - best)
    return (
        best,
        first[1] * left + second[1] * right,
        first[2] * left[..., None] + second[2] * right[..., None],
    )


def shards(
    hidden_in,
    decode_in,
    pre_len,
    new_len,
    key_cache,
    value_cache,
    ln_attn_gain,
    ln_attn_bias,
    ln_mlp_gain,
    ln_mlp_bias,
    qkv_weight,
    qkv_bias,
    out_weight,
    out_bias,
    up_weight,
    up_bias,
    down_weight,
    down_bias,
):
    seqs, new_dev, part_cols = hidden_in.shape
    pre_dev = key_cache.shape[1]
    local_cols = qkv_weight.shape[2]
    heads_dev = local_cols // HD
    width = decode_in.shape[1]
    block_len = pre_dev + new_dev
    rows_new = seqs * new_dev
    ctx_rank = lax.axis_index("ctx")
    tp_rank = lax.axis_index("tp")
    whole = lax.all_gather(hidden_in, "tp", axis=2, tiled=True)
    joined = jnp.concatenate([whole.reshape(rows_new, width), decode_in], axis=0)
    attn_in = norm_rows(joined, ln_attn_gain, ln_attn_bias)
    mlp_in = norm_rows(joined, ln_mlp_gain, ln_mlp_bias)
    proj = [
        jnp.dot(attn_in, qkv_weight[i], preferred_element_type=jnp.float32) + qkv_bias[i]
        for i in range(3)
    ]
    up_act = jax.nn.gelu(
        jnp.dot(mlp_in, up_weight, preferred_element_type=jnp.float32) + up_bias, approximate=False
    ).astype(jnp.bfloat16)
    query_index = ctx_rank * new_dev + jnp.arange(new_dev, dtype=jnp.int32)
    position = pre_len[:, None] + query_index[None, :]
    dec_position = pre_len + new_len
    q_new = rotate(
        proj[0][:rows_new].reshape(seqs, new_dev, heads_dev, HD), position[..., None]
    ).astype(jnp.bfloat16)
    k_new = rotate(
        proj[1][:rows_new].reshape(seqs, new_dev, heads_dev, HD), position[..., None]
    ).astype(jnp.bfloat16)
    v_new = proj[2][:rows_new].reshape(seqs, new_dev, heads_dev, HD).astype(jnp.bfloat16)
    q_dec = rotate(proj[0][rows_new:].reshape(seqs, heads_dev, HD), dec_position[:, None]).astype(
        jnp.bfloat16
    )
    k_dec = rotate(proj[1][rows_new:].reshape(seqs, heads_dev, HD), dec_position[:, None]).astype(
        jnp.bfloat16
    )
    v_dec = proj[2][rows_new:].reshape(seqs, heads_dev, HD).astype(jnp.bfloat16)
    live = query_index[None, :] < new_len[:, None]
    flat_keys = k_new.reshape(seqs, new_dev, local_cols)
    flat_values = v_new.reshape(seqs, new_dev, local_cols)
    new_keys = jnp.where(live[..., None], flat_keys, 0)
    new_values = jnp.where(live[..., None], flat_values, 0)
    local_block = jnp.concatenate(
        [jnp.stack([key_cache, value_cache], axis=2), jnp.stack([flat_keys, flat_values], axis=2)],
        axis=1,
    )
    local_keys = local_block[:, :, 0].reshape(seqs, block_len, heads_dev, HD)
    local_values = local_block[:, :, 1].reshape(seqs, block_len, heads_dev, HD)

    def allowed_for(first, count, queries_at):
        prefix_ok, new_ok, new_pos = key_status(first, count, pre_dev, new_dev, pre_len, new_len)
        return prefix_ok[:, None, :] | new_ok[:, None, :] & (
            new_pos[None, None, :] <= queries_at[None, :, None]
        )

    state = empty_state(seqs, heads_dev, new_dev)
    piece = lax.all_gather(local_block, "ctx", axis=1, tiled=True)
    blocks = piece.shape[1] // block_len

    def one_block(inner, number):
        begin = number * block_len
        slab = lax.dynamic_slice_in_dim(piece, begin, block_len, 1)
        keys = slab[:, :, 0].reshape(seqs, block_len, heads_dev, HD)
        values = slab[:, :, 1].reshape(seqs, block_len, heads_dev, HD)
        allowed = allowed_for(begin, block_len, query_index)
        return (absorb(inner, q_new, keys, values, allowed), None)

    state, _ = lax.scan(one_block, state, jnp.arange(blocks, dtype=jnp.int32))
    top, total, acc = state
    attn_new = (
        (acc / total[..., None])
        .transpose(0, 2, 1, 3)
        .reshape(rows_new, local_cols)
        .astype(jnp.bfloat16)
    )
    prefix_ok, new_ok, new_pos = key_status(
        ctx_rank * block_len, block_len, pre_dev, new_dev, pre_len, new_len
    )
    dec_allowed = (prefix_ok | new_ok)[:, None, :]
    dec_state = absorb(
        empty_state(seqs, heads_dev, 1), q_dec[:, None], local_keys, local_values, dec_allowed
    )
    dec_top, dec_total, dec_acc = joined_2(dec_state, "ctx", join_parts)
    dec_top = dec_top[..., 0]
    dec_total = dec_total[..., 0]
    dec_acc = dec_acc[:, :, 0]
    own = jnp.einsum("shd,shd->sh", q_dec, k_dec, preferred_element_type=jnp.float32) * (
        1.0 / math.sqrt(HD)
    )
    best = jnp.maximum(dec_top, own)
    far_factor = jnp.exp(dec_top - best)
    own_weight = jnp.exp(own - best)
    dec_total = dec_total * far_factor + own_weight
    dec_acc = dec_acc * far_factor[..., None] + jnp.einsum(
        "sh,shd->shd", own_weight.astype(jnp.bfloat16), v_dec, preferred_element_type=jnp.float32
    )
    attn_dec = (dec_acc / dec_total[..., None]).reshape(seqs, local_cols).astype(jnp.bfloat16)
    attn_rows = jnp.concatenate([attn_new, attn_dec], axis=0)
    branches = jnp.dot(attn_rows, out_weight, preferred_element_type=jnp.float32) + jnp.dot(
        up_act, down_weight, preferred_element_type=jnp.float32
    )
    summed_new, summed_dec = (
        lax.psum_scatter(
            branches[:rows_new].reshape(seqs, new_dev, width).astype(jnp.bfloat16),
            "tp",
            scatter_dimension=2,
            tiled=True,
        ).astype(jnp.float32),
        lax.psum_scatter(
            branches[rows_new:].astype(jnp.bfloat16), "tp", scatter_dimension=1, tiled=True
        ).astype(jnp.float32),
    )
    bias = lax.dynamic_slice_in_dim(out_bias + down_bias, tp_rank * part_cols, part_cols)
    prefill = hidden_in.astype(jnp.float32) + summed_new + bias
    prefill_out = jnp.where(live[..., None], prefill, 0.0).astype(jnp.bfloat16)
    dec_resid = lax.dynamic_slice_in_dim(decode_in, tp_rank * part_cols, part_cols, 1)
    decode_out = (dec_resid.astype(jnp.float32) + summed_dec + bias).astype(jnp.bfloat16)
    return (prefill_out, new_keys, new_values, decode_out)


BF = jnp.bfloat16
F32 = jnp.float32
DEC = 16
LSE = 16
SCALE = 1.0 / math.sqrt(HD)


def hop(value, axis, pairs):
    return lax.ppermute(value, axis, pairs)


def call(body, scal, ins, outs, scratch=(), limit=16, after=(), left=()):
    n, m = 1 + len(ins), len(after)

    def run(*refs):
        body(*refs[: n + len(left)], *refs[n + len(left) + m :])

    return pl.pallas_call(
        run,
        out_shape=outs,
        in_specs=[pl.BlockSpec(memory_space=pltpu.SMEM)]
        + [pl.BlockSpec(memory_space=pltpu.VMEM)] * len(ins)
        + [pl.BlockSpec(memory_space=pltpu.HBM)] * len(left)
        + [pl.BlockSpec(memory_space=pl.ANY)] * m,
        out_specs=jax.tree.map(lambda _: pl.BlockSpec(memory_space=pltpu.VMEM), outs),
        scratch_shapes=list(scratch),
        compiler_params=pltpu.CompilerParams(vmem_limit_bytes=limit << 20),
    )(scal, *ins, *left, *after)


def struct(shape, dtype):
    return jax.ShapeDtypeStruct(tuple(shape), dtype)


ME, RANK, PRE, NEW = 0, 1, 2, 2 + DEC


def turn(values, table):
    cosine, down, up = (table[i] for i in range(3))
    parts = []
    for h in range(values.shape[1] // HD):
        one = values[:, h * HD : (h + 1) * HD]
        parts.append(
            one * cosine
            + pltpu.roll(one, HD - ROT // 2, 1) * down
            + pltpu.roll(one, ROT // 2, 1) * up
        )
    return jnp.concatenate(parts, axis=1)


def qkv_body(seqs, rows, part, sc, *refs):
    blocks = refs[:10]
    dec, norms, bias, table, weight = refs[10:15]
    q_out, keys, values, values_t, k_dec, v_dec, mlp_in, attn_in, held, sems = refs[15:]
    copies = [pltpu.make_async_copy(weight.at[i], held.at[i], sems.at[i]) for i in range(3)]
    for copy in copies:
        copy.start()
    me = sc[ME]
    width = part * 8

    def finish(values, base, count, cols):
        total = functools.reduce(lambda a, b: a + b, values)
        mean = jnp.sum(total, axis=-1, keepdims=True) * (1.0 / width)
        values = [v - mean for v in values]
        square = functools.reduce(lambda a, b: a + b, [v * v for v in values])
        spread = jnp.sum(square, axis=-1, keepdims=True) * (1.0 / width)
        inv = lax.rsqrt(spread + EPS)
        for v, col in zip(values, cols, strict=True):
            v = v * inv
            at = pl.ds(col, part)
            attn_in[pl.ds(base, count), at] = (
                v * norms[pl.ds(0, 1), at] + norms[pl.ds(1, 1), at]
            ).astype(BF)
            mlp_in[pl.ds(base, count), at] = (
                v * norms[pl.ds(2, 1), at] + norms[pl.ds(3, 1), at]
            ).astype(BF)

    cols = [pl.multiple_of((me ^ k) * part, part) for k in range(8)]
    for s in range(seqs):
        sources = [blocks[k].at[s] for k in range(6)] + [blocks[6 + s], blocks[8 + s]]

        def step(i, carry):
            at = pl.multiple_of(i * 16, 16)
            values = [ref[pl.ds(at, 16), :].astype(F32) for ref in sources]
            finish(values, pl.multiple_of(s * rows + at, 16), 16, cols)
            return carry

        lax.fori_loop(0, rows // 16, step, 0, unroll=4)
    tokens = [dec[:, pl.ds(k * part, part)].astype(F32) for k in range(8)]
    finish(tokens, seqs * rows, DEC, [k * part for k in range(8)])
    first = sc[RANK] * rows
    slot = lax.broadcasted_iota(jnp.int32, (rows, 1), 0) + first
    outs = []
    for i in range(3):
        copies[i].wait()
        out = jnp.dot(attn_in[...], held[i], preferred_element_type=F32) + bias[pl.ds(i, 1), :]
        if i < 2:
            out = turn(out, table)
        if i == 0:
            q_out[...] = out.astype(BF)
            continue
        for s in range(seqs):
            one = jnp.where(slot < sc[NEW + s], out[s * rows : (s + 1) * rows], 0.0)
            (keys if i == 1 else values)[s] = one.astype(BF)
            if i == 2:
                values_t[s] = jnp.transpose(one).astype(BF)
        (k_dec if i == 1 else v_dec)[...] = out[seqs * rows :].astype(BF)


def qkv(scal, blocks, dec, norms, weight, bias, table, after):
    seqs, rows, part = blocks[0].shape
    _, width, cols = weight.shape
    total = seqs * rows + DEC
    return call(
        functools.partial(qkv_body, seqs, rows, part),
        scal,
        [*blocks, dec, norms, bias, table],
        (
            struct((total, cols), BF),
            *[struct((seqs, rows, cols), BF)] * 2,
            struct((seqs, cols, rows), BF),
            *[struct((DEC, cols), BF)] * 2,
            struct((total, width), BF),
        ),
        scratch=[
            pltpu.VMEM((total, width), BF),
            pltpu.VMEM((3, width, cols), BF),
            pltpu.SemaphoreType.DMA((3,)),
        ],
        limit=32,
        left=[weight],
        after=after,
    )


def attend(query, pieces):
    scores = []
    for keys, _, limit in pieces:
        s = lax.dot_general(query, keys, (((1,), (1,)), ((), ())), preferred_element_type=F32)
        col = lax.broadcasted_iota(jnp.int32, s.shape, 1)
        scores.append(jnp.where(col < limit, s, NEG))
    top = functools.reduce(jnp.maximum, [jnp.max(s, axis=-1, keepdims=True) for s in scores])
    total = 0.0
    acc = 0.0
    for s, (_, values_t, _) in zip(scores, pieces, strict=True):
        weight = jnp.exp2((s - top) * (SCALE * math.log2(math.e)))
        total = total + jnp.sum(weight, axis=-1, keepdims=True)
        acc = acc + lax.dot_general(
            weight.astype(BF), values_t, (((1,), (1,)), ((), ())), preferred_element_type=F32
        )
    return acc / total, top * SCALE + jnp.log(total)


def attend_t(query, pieces):
    scores = []
    for keys, _, limit in pieces:
        s = lax.dot_general(keys, query, (((1,), (1,)), ((), ())), preferred_element_type=F32)
        row = lax.broadcasted_iota(jnp.int32, s.shape, 0)
        scores.append(jnp.where(row < limit, s, NEG))
    top = functools.reduce(jnp.maximum, [jnp.max(s, axis=0, keepdims=True) for s in scores])
    total = 0.0
    acc = 0.0
    for s, (_, values_t, _) in zip(scores, pieces, strict=True):
        weight = jnp.exp2((s - top) * (SCALE * math.log2(math.e)))
        total = total + jnp.sum(weight, axis=0, keepdims=True)
        acc = acc + jnp.dot(values_t, weight.astype(BF), preferred_element_type=F32)
    return acc / total, top * SCALE + jnp.log(total)


def pack_logs(logs):
    logs = jnp.concatenate(logs, axis=0)
    pieces = []
    for _ in range(3):
        short = logs.astype(BF).astype(F32)
        pieces.append(short)
        logs = logs - short
    return jnp.concatenate(pieces + [jnp.zeros_like(logs)], axis=0).astype(BF)


def unpack_logs(tile):
    tile = tile.astype(F32)
    return (tile[0:4] + tile[4:8]) + tile[8:12]


def head_slices(cols):
    return [slice(h * HD, (h + 1) * HD) for h in range(cols // HD)]


def attend_all(q, kc, vc, kn, vn, pre, new):
    found = []
    for at in head_slices(q.shape[1]):
        pieces = [(kc[:, at], vc[at, :], pre), (kn[:, at], vn[at, :], new)]
        found.append(attend_t(q[:, at], pieces))
    return found


def store_partial(out, heads, logs):
    cols = out.shape[0] - LSE
    for at, head in zip(head_slices(cols), heads, strict=True):
        out[at, :] = head.astype(BF)
    out[pl.ds(cols, LSE), :] = pack_logs(logs)


def limits(sc, seq, owner, asker, pre, rows):
    cached = sc[PRE + seq] - owner * pre
    col = lax.broadcasted_iota(jnp.int32, (1, rows), 1)
    fresh = jnp.minimum(sc[NEW + seq] - owner * rows, (asker - owner) * rows + col + 1)
    return cached, fresh


def own_body(seq, rows, pre, sc, q, kc, vc, kn, vn, out):
    rank = sc[RANK]
    found = attend_all(
        q.at[pl.ds(seq * rows, rows)],
        *(a.at[seq] for a in (kc, vc, kn, vn)),
        *limits(sc, seq, rank, rank, pre, rows),
    )
    store_partial(out, *zip(*found, strict=True))


def far_body(seq, rows, pre, sc, q, kc, vc, kn, vn, out):
    rank = sc[RANK]
    found = attend_all(
        q.at[seq],
        *(a.at[seq] for a in (kc, vc, kn, vn)),
        *limits(sc, seq, rank, rank ^ 3, pre, rows),
    )
    store_partial(out, *zip(*found, strict=True))


def attend_one(body, scal, seq, q, kv, after):
    pre, cols = kv[0].shape[1:]
    rows = kv[2].shape[1]
    return call(
        functools.partial(body, seq, rows, pre),
        scal,
        [q, *kv],
        struct((cols + LSE, rows), BF),
        after=after,
    )


def second_body(seq, rows, pre, sc, q, q_far, kc, vc, kn, vn, mine, mine_far, out, out_far):
    rank = sc[RANK]
    cols = kc.shape[1]
    for asker, source, before, target in (
        (rank ^ 3, q_far.at[seq], mine_far, out_far),
        (rank, q.at[pl.ds(seq * rows, rows)], mine, out),
    ):
        found = attend_all(
            source,
            kc,
            vc,
            kn,
            vn,
            *limits(sc, seq, rank ^ 1, asker, pre, rows),
        )
        earlier = unpack_logs(before[pl.ds(cols, LSE), :])
        heads, logs = [], []
        for h, at in enumerate(head_slices(cols)):
            head, log = found[h]
            old = earlier[h : h + 1]
            top = jnp.maximum(log, old)
            a, b = jnp.exp(log - top), jnp.exp(old - top)
            total = a + b
            heads.append((a / total) * head + (b / total) * before[at, :].astype(F32))
            logs.append(top + jnp.log(total))
        store_partial(target, heads, logs)


def attend_second(scal, seq, q, q_far, kv, mine, mine_far, after):
    pre, cols = kv[0].shape
    rows = kv[2].shape[0]
    return call(
        functools.partial(second_body, seq, rows, pre),
        scal,
        [q, q_far, *kv, mine, mine_far],
        (struct((cols + LSE, rows), BF),) * 2,
        after=after,
    )


def dec_body(seqs, rows, pre, sc, q, kc, vc, kn, vn, *refs):
    far, out = refs[:-1], refs[-1]
    rank = sc[RANK]
    row = lax.broadcasted_iota(jnp.int32, (DEC, 1), 0)
    for at in head_slices(kc.shape[2]):
        result = jnp.zeros((DEC, HD), F32)
        log = jnp.full((DEC, HD), NEG, F32)
        for s in range(seqs):
            pieces = []
            mine = (kc.at[s], vc.at[s], kn.at[s], vn.at[s])
            for owner, (k, v, k2, v2) in ((rank, mine), (rank ^ 1, far[4 * s : 4 * s + 4])):
                pieces.append((k[:, at], v[at, :], sc[PRE + s] - owner * pre))
                pieces.append((k2[:, at], v2[at, :], sc[NEW + s] - owner * rows))
            one, one_log = attend(q[pl.ds(seqs * rows, DEC), at], pieces)
            result = jnp.where(row == s, one, result)
            log = jnp.where(row == s, jnp.broadcast_to(one_log, (DEC, HD)), log)
        out[pl.ds(0, DEC), at] = result
        out[pl.ds(DEC, DEC), at] = log


def attend_dec(scal, q, kv, far, after):
    seqs, pre, cols = kv[0].shape
    rows = kv[2].shape[1]
    return call(
        functools.partial(dec_body, seqs, rows, pre),
        scal,
        [q, *kv, *far],
        struct((2 * DEC, cols), F32),
        after=after,
    )


def blend(parts):
    cols = parts[0].shape[0] - LSE
    logs = [unpack_logs(ref[pl.ds(cols, LSE), :]) for ref in parts]
    top = functools.reduce(jnp.maximum, logs)
    weights = [jnp.exp(log - top) for log in logs]
    total = functools.reduce(lambda x, y: x + y, weights)
    heads = []
    for h, at in enumerate(head_slices(cols)):
        acc = 0.0
        for w, ref in zip(weights, parts, strict=True):
            acc = acc + (w / total)[h : h + 1] * ref[at, :].astype(F32)
        heads.append(acc)
    return heads


def decode_body(n, base, sc, q, k, v, *refs):
    parts, out = refs[:n], refs[n]
    for at in head_slices(k.shape[1]):
        both = q[pl.ds(base, DEC), at].astype(F32) * k[:, at].astype(F32)
        own = jnp.broadcast_to(jnp.sum(both, axis=-1, keepdims=True) * SCALE, (DEC, HD))
        logs = [p[pl.ds(DEC, DEC), at] for p in parts]
        top = functools.reduce(jnp.maximum, logs, own)
        share = jnp.exp(own - top)
        total = share
        acc = share.astype(BF).astype(F32) * v[:, at].astype(F32)
        for p, log in zip(parts, logs, strict=True):
            share = jnp.exp(log - top)
            total = total + share
            acc = acc + share * p[pl.ds(0, DEC), at]
        out[:, at] = (acc / total).astype(BF)


def decode_attn(scal, q, k_dec, v_dec, parts, after):
    return call(
        functools.partial(decode_body, len(parts), q.shape[0] - DEC),
        scal,
        [q, k_dec, v_dec, *parts],
        struct(k_dec.shape, BF),
        after=after,
    )


def fetch(weight, held, sems, tile):
    copies = []
    for i in range(weight.shape[1] // tile):
        at = (slice(None), pl.ds(i * tile, tile))
        copies.append(pltpu.make_async_copy(weight.at[at], held.at[at], sems.at[i]))
    for copy in copies:
        copy.start()
    return copies


def up_body(tile, sc, x, bias, weight, out, held, sems):
    for i, copy in enumerate(fetch(weight, held, sems, tile)):
        copy.wait()
        at = slice(i * tile, (i + 1) * tile)
        y = jnp.dot(x[...], held[:, at], preferred_element_type=F32) + bias[:, at]
        out[:, at] = (0.5 * y * (1.0 + lax.erf(y * math.sqrt(0.5)))).astype(BF)


def up_proj(scal, x, weight, bias, after):
    total = x.shape[0]
    width, units = weight.shape
    tile = 512
    return call(
        functools.partial(up_body, tile),
        scal,
        [x, bias],
        struct((total, units), BF),
        scratch=[pltpu.VMEM(weight.shape, BF), pltpu.SemaphoreType.DMA((units // tile,))],
        limit=24,
        left=[weight],
        after=after,
    )


def down_body(tile, sc, x, weight, out, held, sems):
    for i, copy in enumerate(fetch(weight, held, sems, tile)):
        copy.wait()
        at = slice(i * tile, (i + 1) * tile)
        out[:, at] = jnp.dot(x[...], held[:, at], preferred_element_type=F32).astype(BF)


def down_proj(scal, x, weight, after):
    total = x.shape[0]
    units, width = weight.shape
    tile = 1024
    return call(
        functools.partial(down_body, tile),
        scal,
        [x],
        struct((total, width), BF),
        scratch=[pltpu.VMEM(weight.shape, BF), pltpu.SemaphoreType.DMA((width // tile,))],
        limit=24,
        left=[weight],
        after=after,
    )


def place(k):
    return (7 - k) // 2


def out_body(seq, rows, part, sc, mine, far, *refs):
    if seq == 0:
        dec, refs = refs[0], refs[1:]
    weight, mlp, odd, even, attn = refs
    for at, head in zip(head_slices(attn.shape[1]), blend([mine, far]), strict=True):
        attn[pl.ds(0, rows), at] = jnp.transpose(head).astype(BF)
    if seq == 0:
        attn[pl.ds(rows, DEC), :] = dec[...]
    for j in range(8):
        k = sc[ME] ^ j
        at = slice(j * part, (j + 1) * part)
        out = jnp.dot(attn[...], weight[:, at], preferred_element_type=F32)
        base = mlp[pl.ds(seq * rows, rows), at].astype(F32)
        if seq == 0:
            base = jnp.concatenate([base, mlp[pl.ds(mlp.shape[0] - DEC, DEC), at].astype(F32)], axis=0)
        out = (out + base).astype(BF)

        @pl.when(k % 2 == 1)
        def _():
            odd[place(k)] = out

        @pl.when(k % 2 == 0)
        def _():
            even[place(k)] = out


def out_proj(scal, seq, mine, far, dec, weight, mlp, after):
    cols, width = weight.shape
    rows = mine.shape[1]
    part = width // 8
    total = rows + (DEC if seq == 0 else 0)
    return call(
        functools.partial(out_body, seq, rows, part),
        scal,
        [mine, far] + ([dec] if seq == 0 else []) + [weight, mlp],
        (struct((4, total, part), BF),) * 2,
        scratch=[pltpu.VMEM((total, cols), BF)],
        after=after,
    )


def swap(value, bit):
    return hop(value, "tp", [(i, i ^ bit) for i in range(8)])


def gather_rows(own, beside):
    x, y, c = swap(own, 2), swap(own, 4), swap(own, 1)
    x, y, beside = lax.optimization_barrier((x, y, beside))
    da, db = swap(y[0], 2), swap(x[1], 4)
    cx, cy = swap(x, 1), swap(y, 1)
    ca, cb = swap(da, 1), swap(db, 1)
    return [own, c, x, cx, y, cy, da, db, ca, cb], beside


def scatter_rows(odd, even, rows):
    half = rows // 2

    def both(a, b):
        return a.astype(F32) + b.astype(F32)

    other = swap(odd, 1)
    far = both(even[0], other[0]).astype(BF)
    got_y, got_x = swap(far[:half], 2), swap(far[half:], 4)
    to_y = both(even[1], other[1])
    to_y = jnp.concatenate([to_y[:half] + got_y.astype(F32), to_y[half:]], axis=0).astype(BF)
    to_x = both(even[2], other[2])
    to_x = jnp.concatenate([to_x[:half], to_x[half:] + got_x.astype(F32)], axis=0).astype(BF)
    from_x, from_y = swap(to_x, 2), swap(to_y, 4)
    return both(even[3], other[3]) + both(from_x, from_y)


def rope_table(position):
    lane = jnp.arange(HD, dtype=jnp.int32)
    half = ROT // 2
    freqs = jnp.exp((lane % half).astype(F32) * (-2.0 * math.log(10000.0) / ROT))
    angle = position.astype(F32)[:, None] * freqs[None, :]
    cosine = jnp.where(lane < ROT, jnp.cos(angle), 1.0)
    sine = jnp.sin(angle)
    down = jnp.where(lane < half, -sine, 0.0)
    up = jnp.where((lane >= half) & (lane < ROT), sine, 0.0)
    return jnp.stack([cosine, down, up])


def moved_queries(
    hidden_in,
    decode_in,
    pre_len,
    new_len,
    key_cache,
    value_cache,
    ln_attn_gain,
    ln_attn_bias,
    ln_mlp_gain,
    ln_mlp_bias,
    qkv_weight,
    qkv_bias,
    out_weight,
    out_bias,
    up_weight,
    up_bias,
    down_weight,
    down_bias,
):
    seqs, rows, part = hidden_in.shape
    n = lax.axis_size("ctx")
    rank = lax.axis_index("ctx")
    me = lax.axis_index("tp")
    mate = [(i, i ^ 1) for i in range(n)]
    across = [(i, i ^ 3) for i in range(n)]
    room = (0, DEC - seqs)
    scal = jnp.concatenate([jnp.stack([me, rank]), jnp.pad(pre_len, room), jnp.pad(new_len, room)])
    norms = jnp.stack([ln_attn_gain, ln_attn_bias, ln_mlp_gain, ln_mlp_bias])
    dec_rows = jnp.pad(decode_in, (room, (0, 0)))
    index = rank * rows + jnp.arange(rows, dtype=jnp.int32)
    position = [pre_len[s] + index for s in range(seqs)] + [jnp.pad(pre_len + new_len, room)]
    table = rope_table(jnp.concatenate(position))

    values_t = jnp.swapaxes(value_cache, 1, 2)
    far_k = [hop(key_cache[0], "ctx", mate)]
    blocks, (far_k[0], table, dec_rows, norms, later_k, later_v) = gather_rows(
        hidden_in, (far_k[0], table, dec_rows, norms, key_cache[1:], values_t)
    )
    far_k.append(hop(later_k[0], "ctx", mate))
    far_v = [hop(later_v[s], "ctx", mate) for s in range(seqs)]
    q, new_keys, new_values, new_values_t, k_dec, v_dec, mlp_in = qkv(
        scal, blocks, dec_rows, norms, qkv_weight, qkv_bias, table, []
    )
    q_far = hop(q[: seqs * rows].reshape(seqs, rows, -1), "ctx", across)
    kv = (key_cache, values_t, new_keys, new_values_t)
    pairs = [
        (far_k[s], far_v[s], hop(new_keys[s], "ctx", mate), hop(new_values_t[s], "ctx", mate))
        for s in range(seqs)
    ]

    own = [attend_one(own_body, scal, 0, q, kv, [far_k[1], far_v[0]])]
    own.append(attend_one(own_body, scal, 1, q, kv, [own[0]]))
    up = up_proj(scal, mlp_in, up_weight, up_bias[None, :], [own[1], far_v[1]])
    last = up
    ends = []
    for s in range(seqs):
        far = attend_one(far_body, scal, s, q_far, kv, [last])
        mine, back = attend_second(scal, s, q, q_far, pairs[s], own[s], far, [])
        last = back
        ends.append((mine, hop(back, "ctx", across)))
    dec = attend_dec(scal, q, kv, [*pairs[0], *pairs[1]], [last])
    dec_far = hop(dec, "ctx", across)
    mlp = down_proj(scal, up, down_weight, [dec])
    attn_dec = decode_attn(scal, q, k_dec, v_dec, [dec, dec_far], [mlp])
    last = attn_dec

    bias = lax.dynamic_slice_in_dim(out_bias + down_bias, me * part, part)
    prefill = []
    for s in range(seqs):
        odd, even = out_proj(
            scal, s, *ends[s], attn_dec if s == 0 else None, out_weight, mlp, [last]
        )
        last = even
        summed = scatter_rows(odd, even, rows)
        live = index < new_len[s]
        full = hidden_in[s].astype(F32) + summed[:rows] + bias
        prefill.append(jnp.where(live[:, None], full, 0.0).astype(BF))
        if s == 0:
            resid = lax.dynamic_slice_in_dim(decode_in, me * part, part, 1)
            decode_out = (resid.astype(F32) + summed[rows : rows + seqs] + bias).astype(BF)
    return (jnp.stack(prefill), new_keys, new_values, decode_out)


def layer(ctx, tp, *args):
    seqs, rows, part = args[0].shape
    pre, cols = args[4].shape[1:]
    if tp == 8 and ctx == 4 and seqs == 2 and rows % HD == 0 and pre % HD == 0 and cols == 4 * HD:
        return moved_queries(*args)
    return shards(*args)


def solution(mesh):
    return jax.shard_map(
        functools.partial(layer, mesh.shape["ctx"], mesh.shape["tp"]),
        mesh=mesh,
        in_specs=(
            P(None, "ctx", "tp"),
            P(),
            P(),
            P(),
            P(None, "ctx", "tp"),
            P(None, "ctx", "tp"),
            P(),
            P(),
            P(),
            P(),
            P(None, None, "tp"),
            P(None, "tp"),
            P("tp", None),
            P(),
            P(None, "tp"),
            P("tp"),
            P("tp", None),
            P(),
        ),
        out_specs=(P(None, "ctx", "tp"), P(None, "ctx", "tp"), P(None, "ctx", "tp"), P(None, "tp")),
        check_vma=False,
    )
```

```python
import functools
import math

import jax
import jax.numpy as jnp
from jax import lax
from jax.experimental import pallas as pl
from jax.experimental.pallas import tpu as pltpu
from jax.sharding import PartitionSpec as P

HD = 128
ROT = 32


EPS = 1e-05
NEG = -1e30


def joined_2(part, axis, combine):
    gathered = jax.tree.map(lambda a: lax.all_gather(a, axis), part)

    def take(source):
        return jax.tree.map(lambda a: lax.dynamic_index_in_dim(a, source, 0, False), gathered)

    return lax.fori_loop(
        1, lax.axis_size(axis), lambda source, state: combine(state, take(source)), take(0)
    )


def norm_rows(rows, gain, shift):
    values = rows.astype(jnp.float32)
    center = values - jnp.mean(values, axis=-1, keepdims=True)
    spread = jnp.mean(center * center, axis=-1, keepdims=True)
    return (center * lax.rsqrt(spread + EPS) * gain + shift).astype(jnp.bfloat16)


def rotate(values, position):
    half = ROT // 2
    freqs = jnp.exp(jnp.arange(half, dtype=jnp.float32) * (-2.0 * math.log(10000.0) / ROT))
    angle = position.astype(jnp.float32)[..., None] * freqs
    cosine = jnp.cos(angle)
    sine = jnp.sin(angle)
    first = values[..., :half]
    second = values[..., half:ROT]
    return jnp.concatenate(
        [first * cosine - second * sine, second * cosine + first * sine, values[..., ROT:]], axis=-1
    )


def key_status(first, count, pre_dev, new_dev, pre_len, new_len):
    index = first + jnp.arange(count, dtype=jnp.int32)
    owner = index // (pre_dev + new_dev)
    offset = index % (pre_dev + new_dev)
    is_prefix = offset < pre_dev
    prefix_pos = owner * pre_dev + offset
    new_pos = owner * new_dev + offset - pre_dev
    prefix_ok = is_prefix[None, :] & (prefix_pos[None, :] < pre_len[:, None])
    new_ok = jnp.logical_not(is_prefix)[None, :] & (new_pos[None, :] < new_len[:, None])
    return (prefix_ok, new_ok, new_pos)


def absorb(state, queries, keys, values, allowed):
    top, total, acc = state
    scores = jnp.einsum("sqhd,skhd->shqk", queries, keys, preferred_element_type=jnp.float32) * (
        1.0 / math.sqrt(HD)
    )
    mask = allowed[:, None]
    scores = jnp.where(mask, scores, NEG)
    new_top = jnp.maximum(top, jnp.max(scores, axis=-1))
    weight = jnp.where(mask, jnp.exp(scores - new_top[..., None]), 0.0)
    factor = jnp.exp(top - new_top)
    total = total * factor + jnp.sum(weight, axis=-1)
    acc = acc * factor[..., None] + jnp.einsum(
        "shqk,skhd->shqd", weight.astype(jnp.bfloat16), values, preferred_element_type=jnp.float32
    )
    return (new_top, total, acc)


def empty_state(seqs, heads_dev, count):
    return (
        jnp.full((seqs, heads_dev, count), NEG, jnp.float32),
        jnp.zeros((seqs, heads_dev, count), jnp.float32),
        jnp.zeros((seqs, heads_dev, count, HD), jnp.float32),
    )


def join_parts(first, second):
    best = jnp.maximum(first[0], second[0])
    left = jnp.exp(first[0] - best)
    right = jnp.exp(second[0] - best)
    return (
        best,
        first[1] * left + second[1] * right,
        first[2] * left[..., None] + second[2] * right[..., None],
    )


def shards(
    hidden_in,
    decode_in,
    pre_len,
    new_len,
    key_cache,
    value_cache,
    ln_attn_gain,
    ln_attn_bias,
    ln_mlp_gain,
    ln_mlp_bias,
    qkv_weight,
    qkv_bias,
    out_weight,
    out_bias,
    up_weight,
    up_bias,
    down_weight,
    down_bias,
):
    seqs, new_dev, part_cols = hidden_in.shape
    pre_dev = key_cache.shape[1]
    local_cols = qkv_weight.shape[2]
    heads_dev = local_cols // HD
    width = decode_in.shape[1]
    block_len = pre_dev + new_dev
    rows_new = seqs * new_dev
    ctx_rank = lax.axis_index("ctx")
    tp_rank = lax.axis_index("tp")
    whole = lax.all_gather(hidden_in, "tp", axis=2, tiled=True)
    joined = jnp.concatenate([whole.reshape(rows_new, width), decode_in], axis=0)
    attn_in = norm_rows(joined, ln_attn_gain, ln_attn_bias)
    mlp_in = norm_rows(joined, ln_mlp_gain, ln_mlp_bias)
    proj = [
        jnp.dot(attn_in, qkv_weight[i], preferred_element_type=jnp.float32) + qkv_bias[i]
        for i in range(3)
    ]
    up_act = jax.nn.gelu(
        jnp.dot(mlp_in, up_weight, preferred_element_type=jnp.float32) + up_bias, approximate=False
    ).astype(jnp.bfloat16)
    query_index = ctx_rank * new_dev + jnp.arange(new_dev, dtype=jnp.int32)
    position = pre_len[:, None] + query_index[None, :]
    dec_position = pre_len + new_len
    q_new = rotate(
        proj[0][:rows_new].reshape(seqs, new_dev, heads_dev, HD), position[..., None]
    ).astype(jnp.bfloat16)
    k_new = rotate(
        proj[1][:rows_new].reshape(seqs, new_dev, heads_dev, HD), position[..., None]
    ).astype(jnp.bfloat16)
    v_new = proj[2][:rows_new].reshape(seqs, new_dev, heads_dev, HD).astype(jnp.bfloat16)
    q_dec = rotate(proj[0][rows_new:].reshape(seqs, heads_dev, HD), dec_position[:, None]).astype(
        jnp.bfloat16
    )
    k_dec = rotate(proj[1][rows_new:].reshape(seqs, heads_dev, HD), dec_position[:, None]).astype(
        jnp.bfloat16
    )
    v_dec = proj[2][rows_new:].reshape(seqs, heads_dev, HD).astype(jnp.bfloat16)
    live = query_index[None, :] < new_len[:, None]
    flat_keys = k_new.reshape(seqs, new_dev, local_cols)
    flat_values = v_new.reshape(seqs, new_dev, local_cols)
    new_keys = jnp.where(live[..., None], flat_keys, 0)
    new_values = jnp.where(live[..., None], flat_values, 0)
    local_block = jnp.concatenate(
        [jnp.stack([key_cache, value_cache], axis=2), jnp.stack([flat_keys, flat_values], axis=2)],
        axis=1,
    )
    local_keys = local_block[:, :, 0].reshape(seqs, block_len, heads_dev, HD)
    local_values = local_block[:, :, 1].reshape(seqs, block_len, heads_dev, HD)

    def allowed_for(first, count, queries_at):
        prefix_ok, new_ok, new_pos = key_status(first, count, pre_dev, new_dev, pre_len, new_len)
        return prefix_ok[:, None, :] | new_ok[:, None, :] & (
            new_pos[None, None, :] <= queries_at[None, :, None]
        )

    state = empty_state(seqs, heads_dev, new_dev)
    piece = lax.all_gather(local_block, "ctx", axis=1, tiled=True)
    blocks = piece.shape[1] // block_len

    def one_block(inner, number):
        begin = number * block_len
        slab = lax.dynamic_slice_in_dim(piece, begin, block_len, 1)
        keys = slab[:, :, 0].reshape(seqs, block_len, heads_dev, HD)
        values = slab[:, :, 1].reshape(seqs, block_len, heads_dev, HD)
        allowed = allowed_for(begin, block_len, query_index)
        return (absorb(inner, q_new, keys, values, allowed), None)

    state, _ = lax.scan(one_block, state, jnp.arange(blocks, dtype=jnp.int32))
    top, total, acc = state
    attn_new = (
        (acc / total[..., None])
        .transpose(0, 2, 1, 3)
        .reshape(rows_new, local_cols)
        .astype(jnp.bfloat16)
    )
    prefix_ok, new_ok, new_pos = key_status(
        ctx_rank * block_len, block_len, pre_dev, new_dev, pre_len, new_len
    )
    dec_allowed = (prefix_ok | new_ok)[:, None, :]
    dec_state = absorb(
        empty_state(seqs, heads_dev, 1), q_dec[:, None], local_keys, local_values, dec_allowed
    )
    dec_top, dec_total, dec_acc = joined_2(dec_state, "ctx", join_parts)
    dec_top = dec_top[..., 0]
    dec_total = dec_total[..., 0]
    dec_acc = dec_acc[:, :, 0]
    own = jnp.einsum("shd,shd->sh", q_dec, k_dec, preferred_element_type=jnp.float32) * (
        1.0 / math.sqrt(HD)
    )
    best = jnp.maximum(dec_top, own)
    far_factor = jnp.exp(dec_top - best)
    own_weight = jnp.exp(own - best)
    dec_total = dec_total * far_factor + own_weight
    dec_acc = dec_acc * far_factor[..., None] + jnp.einsum(
        "sh,shd->shd", own_weight.astype(jnp.bfloat16), v_dec, preferred_element_type=jnp.float32
    )
    attn_dec = (dec_acc / dec_total[..., None]).reshape(seqs, local_cols).astype(jnp.bfloat16)
    attn_rows = jnp.concatenate([attn_new, attn_dec], axis=0)
    branches = jnp.dot(attn_rows, out_weight, preferred_element_type=jnp.float32) + jnp.dot(
        up_act, down_weight, preferred_element_type=jnp.float32
    )
    summed_new, summed_dec = (
        lax.psum_scatter(
            branches[:rows_new].reshape(seqs, new_dev, width).astype(jnp.bfloat16),
            "tp",
            scatter_dimension=2,
            tiled=True,
        ).astype(jnp.float32),
        lax.psum_scatter(
            branches[rows_new:].astype(jnp.bfloat16), "tp", scatter_dimension=1, tiled=True
        ).astype(jnp.float32),
    )
    bias = lax.dynamic_slice_in_dim(out_bias + down_bias, tp_rank * part_cols, part_cols)
    prefill = hidden_in.astype(jnp.float32) + summed_new + bias
    prefill_out = jnp.where(live[..., None], prefill, 0.0).astype(jnp.bfloat16)
    dec_resid = lax.dynamic_slice_in_dim(decode_in, tp_rank * part_cols, part_cols, 1)
    decode_out = (dec_resid.astype(jnp.float32) + summed_dec + bias).astype(jnp.bfloat16)
    return (prefill_out, new_keys, new_values, decode_out)


BF = jnp.bfloat16
F32 = jnp.float32
DEC = 16
LSE = 16
SCALE = 1.0 / math.sqrt(HD)


def hop(value, axis, pairs):
    return lax.ppermute(value, axis, pairs)


def call(body, scal, ins, outs, scratch=(), limit=16, after=(), left=()):
    n, m = 1 + len(ins), len(after)
    left = [pltpu.with_memory_space_constraint(a, pltpu.HBM) for a in left]

    def run(*refs):
        body(*refs[: n + len(left)], *refs[n + len(left) + m :])

    return pl.pallas_call(
        run,
        out_shape=outs,
        in_specs=[pl.BlockSpec(memory_space=pltpu.SMEM)]
        + [pl.BlockSpec(memory_space=pltpu.VMEM)] * len(ins)
        + [pl.BlockSpec(memory_space=pltpu.HBM)] * len(left)
        + [pl.BlockSpec(memory_space=pl.ANY)] * m,
        out_specs=jax.tree.map(lambda _: pl.BlockSpec(memory_space=pltpu.VMEM), outs),
        scratch_shapes=list(scratch),
        compiler_params=pltpu.CompilerParams(vmem_limit_bytes=limit << 20),
    )(scal, *ins, *left, *after)


def struct(shape, dtype):
    return jax.ShapeDtypeStruct(tuple(shape), dtype)


ME, RANK, PRE, NEW = 0, 1, 2, 2 + DEC


def turn(values, table):
    cosine, down, up = (table[i] for i in range(3))
    parts = []
    for h in range(values.shape[1] // HD):
        one = values[:, h * HD : (h + 1) * HD]
        parts.append(
            one * cosine
            + pltpu.roll(one, HD - ROT // 2, 1) * down
            + pltpu.roll(one, ROT // 2, 1) * up
        )
    return jnp.concatenate(parts, axis=1)


def qkv_body(seqs, rows, part, sc, dec, norms, bias, table, *refs):
    weight, blocks = refs[0], refs[1:11]
    q_out, keys, values, values_t, k_dec, v_dec, mlp_in = refs[11:18]
    attn_in, held, hidden, sems, block_sems = refs[18:]
    moves = []
    for s in range(seqs):
        sources = [blocks[k].at[s] for k in range(6)] + [blocks[6 + s], blocks[8 + s]]
        moves.append(
            [
                pltpu.make_async_copy(source, hidden.at[s, k], block_sems.at[s, k])
                for k, source in enumerate(sources)
            ]
        )
        for move in moves[s]:
            move.start()
    copies = [pltpu.make_async_copy(weight.at[i], held.at[i], sems.at[i]) for i in range(3)]
    for copy in copies:
        copy.start()
    me = sc[ME]
    width = part * 8

    def finish(values, base, count, cols):
        total = functools.reduce(lambda a, b: a + b, values)
        mean = jnp.sum(total, axis=-1, keepdims=True) * (1.0 / width)
        values = [v - mean for v in values]
        square = functools.reduce(lambda a, b: a + b, [v * v for v in values])
        spread = jnp.sum(square, axis=-1, keepdims=True) * (1.0 / width)
        inv = lax.rsqrt(spread + EPS)
        for v, col in zip(values, cols, strict=True):
            v = v * inv
            at = pl.ds(col, part)
            attn_in[pl.ds(base, count), at] = (
                v * norms[pl.ds(0, 1), at] + norms[pl.ds(1, 1), at]
            ).astype(BF)
            mlp_in[pl.ds(base, count), at] = (
                v * norms[pl.ds(2, 1), at] + norms[pl.ds(3, 1), at]
            ).astype(BF)

    cols = [pl.multiple_of((me ^ k) * part, part) for k in range(8)]
    for s in range(seqs):
        for move in moves[s]:
            move.wait()

        def step(i, carry):
            at = pl.multiple_of(i * 16, 16)
            rows_of = [hidden[s, k, pl.ds(at, 16), :].astype(F32) for k in range(8)]
            finish(rows_of, pl.multiple_of(s * rows + at, 16), 16, cols)
            return carry

        lax.fori_loop(0, rows // 16, step, 0, unroll=4)
    tokens = [dec[:, pl.ds(k * part, part)].astype(F32) for k in range(8)]
    finish(tokens, seqs * rows, DEC, [k * part for k in range(8)])
    first = sc[RANK] * rows
    slot = lax.broadcasted_iota(jnp.int32, (rows, 1), 0) + first
    outs = []
    for i in range(3):
        copies[i].wait()
        out = jnp.dot(attn_in[...], held[i], preferred_element_type=F32) + bias[pl.ds(i, 1), :]
        if i < 2:
            out = turn(out, table)
        if i == 0:
            q_out[...] = out.astype(BF)
            continue
        for s in range(seqs):
            one = jnp.where(slot < sc[NEW + s], out[s * rows : (s + 1) * rows], 0.0)
            (keys if i == 1 else values)[s] = one.astype(BF)
            if i == 2:
                values_t[s] = jnp.transpose(one).astype(BF)
        (k_dec if i == 1 else v_dec)[...] = out[seqs * rows :].astype(BF)


def qkv(scal, blocks, dec, norms, weight, bias, table, after):
    seqs, rows, part = blocks[0].shape
    _, width, cols = weight.shape
    total = seqs * rows + DEC
    return call(
        functools.partial(qkv_body, seqs, rows, part),
        scal,
        [dec, norms, bias, table],
        (
            struct((total, cols), BF),
            *[struct((seqs, rows, cols), BF)] * 2,
            struct((seqs, cols, rows), BF),
            *[struct((DEC, cols), BF)] * 2,
            struct((total, width), BF),
        ),
        scratch=[
            pltpu.VMEM((total, width), BF),
            pltpu.VMEM((3, width, cols), BF),
            pltpu.VMEM((seqs, 8, rows, part), BF),
            pltpu.SemaphoreType.DMA((3,)),
            pltpu.SemaphoreType.DMA((seqs, 8)),
        ],
        limit=32,
        left=[weight, *blocks],
        after=after,
    )


def attend(query, pieces):
    scores = []
    for keys, _, limit in pieces:
        s = lax.dot_general(query, keys, (((1,), (1,)), ((), ())), preferred_element_type=F32)
        col = lax.broadcasted_iota(jnp.int32, s.shape, 1)
        scores.append(jnp.where(col < limit, s, NEG))
    top = functools.reduce(jnp.maximum, [jnp.max(s, axis=-1, keepdims=True) for s in scores])
    total = 0.0
    acc = 0.0
    for s, (_, values_t, _) in zip(scores, pieces, strict=True):
        weight = jnp.exp2((s - top) * (SCALE * math.log2(math.e)))
        total = total + jnp.sum(weight, axis=-1, keepdims=True)
        acc = acc + lax.dot_general(
            weight.astype(BF), values_t, (((1,), (1,)), ((), ())), preferred_element_type=F32
        )
    return acc / total, top * SCALE + jnp.log(total)


def attend_t(query, pieces):
    scores = []
    for keys, _, limit in pieces:
        s = lax.dot_general(keys, query, (((1,), (1,)), ((), ())), preferred_element_type=F32)
        row = lax.broadcasted_iota(jnp.int32, s.shape, 0)
        scores.append(jnp.where(row < limit, s, NEG))
    top = functools.reduce(jnp.maximum, [jnp.max(s, axis=0, keepdims=True) for s in scores])
    total = 0.0
    acc = 0.0
    for s, (_, values_t, _) in zip(scores, pieces, strict=True):
        weight = jnp.exp2((s - top) * (SCALE * math.log2(math.e)))
        total = total + jnp.sum(weight, axis=0, keepdims=True)
        acc = acc + jnp.dot(values_t, weight.astype(BF), preferred_element_type=F32)
    return acc / total, top * SCALE + jnp.log(total)


def pack_logs(logs):
    logs = jnp.concatenate(logs, axis=0)
    pieces = []
    for _ in range(3):
        short = logs.astype(BF).astype(F32)
        pieces.append(short)
        logs = logs - short
    return jnp.concatenate(pieces + [jnp.zeros_like(logs)], axis=0).astype(BF)


def unpack_logs(tile):
    tile = tile.astype(F32)
    return (tile[0:4] + tile[4:8]) + tile[8:12]


def head_slices(cols):
    return [slice(h * HD, (h + 1) * HD) for h in range(cols // HD)]


def attend_all(q, kc, vc, kn, vn, pre, new):
    found = []
    for at in head_slices(q.shape[1]):
        pieces = [(kc[:, at], vc[at, :], pre), (kn[:, at], vn[at, :], new)]
        found.append(attend_t(q[:, at], pieces))
    return found


def store_partial(out, heads, logs):
    cols = out.shape[0] - LSE
    for at, head in zip(head_slices(cols), heads, strict=True):
        out[at, :] = head.astype(BF)
    out[pl.ds(cols, LSE), :] = pack_logs(logs)


def limits(sc, seq, owner, asker, pre, rows):
    cached = sc[PRE + seq] - owner * pre
    col = lax.broadcasted_iota(jnp.int32, (1, rows), 1)
    fresh = jnp.minimum(sc[NEW + seq] - owner * rows, (asker - owner) * rows + col + 1)
    return cached, fresh


def own_body(seq, rows, pre, sc, q, kc, vc, kn, vn, out):
    rank = sc[RANK]
    found = attend_all(
        q.at[pl.ds(seq * rows, rows)],
        *(a.at[seq] for a in (kc, vc, kn, vn)),
        *limits(sc, seq, rank, rank, pre, rows),
    )
    store_partial(out, *zip(*found, strict=True))


def far_body(seq, rows, pre, sc, q, kc, vc, kn, vn, out):
    rank = sc[RANK]
    found = attend_all(
        q.at[seq],
        *(a.at[seq] for a in (kc, vc, kn, vn)),
        *limits(sc, seq, rank, rank ^ 3, pre, rows),
    )
    store_partial(out, *zip(*found, strict=True))


def attend_one(body, scal, seq, q, kv, after):
    pre, cols = kv[0].shape[1:]
    rows = kv[2].shape[1]
    return call(
        functools.partial(body, seq, rows, pre),
        scal,
        [q, *kv],
        struct((cols + LSE, rows), BF),
        after=after,
    )


def second_body(seq, rows, pre, sc, q, q_far, kc, vc, kn, vn, mine, mine_far, out, out_far):
    rank = sc[RANK]
    cols = kc.shape[2]
    for asker, source, before, target in (
        (rank ^ 3, q_far.at[seq], mine_far, out_far),
        (rank, q.at[pl.ds(seq * rows, rows)], mine, out),
    ):
        found = attend_all(
            source,
            kc.at[seq],
            vc.at[seq],
            kn.at[seq],
            vn.at[seq],
            *limits(sc, seq, rank ^ 1, asker, pre, rows),
        )
        earlier = unpack_logs(before[pl.ds(cols, LSE), :])
        heads, logs = [], []
        for h, at in enumerate(head_slices(cols)):
            head, log = found[h]
            old = earlier[h : h + 1]
            top = jnp.maximum(log, old)
            a, b = jnp.exp(log - top), jnp.exp(old - top)
            total = a + b
            heads.append((a / total) * head + (b / total) * before[at, :].astype(F32))
            logs.append(top + jnp.log(total))
        store_partial(target, heads, logs)


def attend_second(scal, seq, q, q_far, kv, mine, mine_far, after):
    pre, cols = kv[0].shape[1:]
    rows = kv[2].shape[1]
    return call(
        functools.partial(second_body, seq, rows, pre),
        scal,
        [q, q_far, *kv, mine, mine_far],
        (struct((cols + LSE, rows), BF),) * 2,
        after=after,
    )


def dec_body(seqs, rows, pre, sc, q, kc, vc, kn, vn, *refs):
    far, out = refs[:-1], refs[-1]
    far = [[a.at[s] for a in far] for s in range(seqs)]
    rank = sc[RANK]
    row = lax.broadcasted_iota(jnp.int32, (DEC, 1), 0)
    for at in head_slices(kc.shape[2]):
        result = jnp.zeros((DEC, HD), F32)
        log = jnp.full((DEC, HD), NEG, F32)
        for s in range(seqs):
            pieces = []
            mine = (kc.at[s], vc.at[s], kn.at[s], vn.at[s])
            for owner, (k, v, k2, v2) in ((rank, mine), (rank ^ 1, far[s])):
                pieces.append((k[:, at], v[at, :], sc[PRE + s] - owner * pre))
                pieces.append((k2[:, at], v2[at, :], sc[NEW + s] - owner * rows))
            one, one_log = attend(q[pl.ds(seqs * rows, DEC), at], pieces)
            result = jnp.where(row == s, one, result)
            log = jnp.where(row == s, jnp.broadcast_to(one_log, (DEC, HD)), log)
        out[pl.ds(0, DEC), at] = result
        out[pl.ds(DEC, DEC), at] = log


def attend_dec(scal, q, kv, far, after):
    seqs, pre, cols = kv[0].shape
    rows = kv[2].shape[1]
    return call(
        functools.partial(dec_body, seqs, rows, pre),
        scal,
        [q, *kv, *far],
        struct((2 * DEC, cols), F32),
        after=after,
    )


def blend(parts):
    cols = parts[0].shape[0] - LSE
    logs = [unpack_logs(ref[pl.ds(cols, LSE), :]) for ref in parts]
    top = functools.reduce(jnp.maximum, logs)
    weights = [jnp.exp(log - top) for log in logs]
    total = functools.reduce(lambda x, y: x + y, weights)
    heads = []
    for h, at in enumerate(head_slices(cols)):
        acc = 0.0
        for w, ref in zip(weights, parts, strict=True):
            acc = acc + (w / total)[h : h + 1] * ref[at, :].astype(F32)
        heads.append(acc)
    return heads


def decode_body(n, base, sc, q, k, v, *refs):
    parts, out = refs[:n], refs[n]
    for at in head_slices(k.shape[1]):
        both = q[pl.ds(base, DEC), at].astype(F32) * k[:, at].astype(F32)
        own = jnp.broadcast_to(jnp.sum(both, axis=-1, keepdims=True) * SCALE, (DEC, HD))
        logs = [p[pl.ds(DEC, DEC), at] for p in parts]
        top = functools.reduce(jnp.maximum, logs, own)
        share = jnp.exp(own - top)
        total = share
        acc = share.astype(BF).astype(F32) * v[:, at].astype(F32)
        for p, log in zip(parts, logs, strict=True):
            share = jnp.exp(log - top)
            total = total + share
            acc = acc + share * p[pl.ds(0, DEC), at]
        out[:, at] = (acc / total).astype(BF)


def decode_attn(scal, q, k_dec, v_dec, parts, after):
    return call(
        functools.partial(decode_body, len(parts), q.shape[0] - DEC),
        scal,
        [q, k_dec, v_dec, *parts],
        struct(k_dec.shape, BF),
        after=after,
    )


def fetch(weight, held, sems, tile):
    copies = []
    for i in range(weight.shape[1] // tile):
        at = (slice(None), pl.ds(i * tile, tile))
        copies.append(pltpu.make_async_copy(weight.at[at], held.at[at], sems.at[i]))
    for copy in copies:
        copy.start()
    return copies


def up_body(tile, sc, x, bias, weight, out, held, sems):
    fetch(weight, held, sems, tile)

    def step(i, carry):
        at = (slice(None), pl.ds(pl.multiple_of(i * tile, tile), tile))
        pltpu.make_async_copy(weight.at[at], held.at[at], sems.at[i]).wait()
        y = jnp.dot(x[...], held[at], preferred_element_type=F32) + bias[at]
        out[at] = (0.5 * y * (1.0 + lax.erf(y * math.sqrt(0.5)))).astype(BF)
        return carry

    lax.fori_loop(0, weight.shape[1] // tile, step, 0)


def up_proj(scal, x, weight, bias, after):
    total = x.shape[0]
    width, units = weight.shape
    tile = 512
    return call(
        functools.partial(up_body, tile),
        scal,
        [x, bias],
        struct((total, units), BF),
        scratch=[pltpu.VMEM(weight.shape, BF), pltpu.SemaphoreType.DMA((units // tile,))],
        limit=24,
        left=[weight],
        after=after,
    )


def down_body(tile, sc, x, weight, out, held, sems):
    for i, copy in enumerate(fetch(weight, held, sems, tile)):
        copy.wait()
        at = slice(i * tile, (i + 1) * tile)
        out[:, at] = jnp.dot(x[...], held[:, at], preferred_element_type=F32).astype(BF)


def down_proj(scal, x, weight, after):
    total = x.shape[0]
    units, width = weight.shape
    tile = 1024
    return call(
        functools.partial(down_body, tile),
        scal,
        [x],
        struct((total, width), BF),
        scratch=[pltpu.VMEM(weight.shape, BF), pltpu.SemaphoreType.DMA((width // tile,))],
        limit=24,
        left=[weight],
        after=after,
    )


def place(k):
    return (7 - k) // 2


def out_body(seq, tail, rows, part, sc, mine, far, *refs):
    if tail:
        dec, refs = refs[0], refs[1:]
    weight, mlp, odd, even, attn = refs
    for at, head in zip(head_slices(attn.shape[1]), blend([mine, far]), strict=True):
        attn[pl.ds(0, rows), at] = jnp.transpose(head).astype(BF)
    if tail:
        attn[pl.ds(rows, DEC), :] = dec[...]
    for j in range(8):
        k = sc[ME] ^ j
        at = slice(j * part, (j + 1) * part)
        out = jnp.dot(attn[...], weight[:, at], preferred_element_type=F32)
        base = mlp[pl.ds(seq * rows, rows), at].astype(F32)
        if tail:
            base = jnp.concatenate([base, mlp[pl.ds(mlp.shape[0] - DEC, DEC), at].astype(F32)], axis=0)
        out = (out + base).astype(BF)

        @pl.when(k % 2 == 1)
        def _():
            odd[place(k)] = out

        @pl.when(k % 2 == 0)
        def _():
            even[place(k)] = out


def out_proj(scal, seq, mine, far, dec, weight, mlp, after):
    cols, width = weight.shape
    rows = mine.shape[1]
    part = width // 8
    tail = dec is not None
    total = rows + (DEC if tail else 0)
    return call(
        functools.partial(out_body, seq, tail, rows, part),
        scal,
        [mine, far] + ([dec] if tail else []) + [weight, mlp],
        (struct((4, total, part), BF),) * 2,
        scratch=[pltpu.VMEM((total, cols), BF)],
        after=after,
    )


def swap(value, bit):
    return hop(value, "tp", [(i, i ^ bit) for i in range(8)])


def gather_rows(own, beside):
    x, y, c = swap(own, 2), swap(own, 4), swap(own, 1)
    x, y, beside = lax.optimization_barrier((x, y, beside))
    da, db = swap(y[0], 2), swap(x[1], 4)
    cx, cy = swap(x, 1), swap(y, 1)
    ca, cb = swap(da, 1), swap(db, 1)
    return [own, c, x, cx, y, cy, da, db, ca, cb], beside


def scatter_rows(odd, even, rows):
    half = rows // 2

    def both(a, b):
        return a.astype(F32) + b.astype(F32)

    other = swap(odd, 1)
    far = both(even[0], other[0]).astype(BF)
    got_y, got_x = swap(far[:half], 2), swap(far[half:], 4)
    to_y = both(even[1], other[1])
    to_y = jnp.concatenate([to_y[:half] + got_y.astype(F32), to_y[half:]], axis=0).astype(BF)
    to_x = both(even[2], other[2])
    to_x = jnp.concatenate([to_x[:half], to_x[half:] + got_x.astype(F32)], axis=0).astype(BF)
    from_x, from_y = swap(to_x, 2), swap(to_y, 4)
    return both(even[3], other[3]) + both(from_x, from_y)


def rope_table(position):
    lane = jnp.arange(HD, dtype=jnp.int32)
    half = ROT // 2
    freqs = jnp.exp((lane % half).astype(F32) * (-2.0 * math.log(10000.0) / ROT))
    angle = position.astype(F32)[:, None] * freqs[None, :]
    cosine = jnp.where(lane < ROT, jnp.cos(angle), 1.0)
    sine = jnp.sin(angle)
    down = jnp.where(lane < half, -sine, 0.0)
    up = jnp.where((lane >= half) & (lane < ROT), sine, 0.0)
    return jnp.stack([cosine, down, up])


def moved_queries(
    hidden_in,
    decode_in,
    pre_len,
    new_len,
    key_cache,
    value_cache,
    ln_attn_gain,
    ln_attn_bias,
    ln_mlp_gain,
    ln_mlp_bias,
    qkv_weight,
    qkv_bias,
    out_weight,
    out_bias,
    up_weight,
    up_bias,
    down_weight,
    down_bias,
):
    seqs, rows, part = hidden_in.shape
    n = lax.axis_size("ctx")
    rank = lax.axis_index("ctx")
    me = lax.axis_index("tp")
    mate = [(i, i ^ 1) for i in range(n)]
    across = [(i, i ^ 3) for i in range(n)]
    room = (0, DEC - seqs)
    scal = jnp.concatenate([jnp.stack([me, rank]), jnp.pad(pre_len, room), jnp.pad(new_len, room)])
    norms = jnp.stack([ln_attn_gain, ln_attn_bias, ln_mlp_gain, ln_mlp_bias])
    dec_rows = jnp.pad(decode_in, (room, (0, 0)))
    index = rank * rows + jnp.arange(rows, dtype=jnp.int32)
    position = [pre_len[s] + index for s in range(seqs)] + [jnp.pad(pre_len + new_len, room)]
    table = rope_table(jnp.concatenate(position))

    values_t = jnp.swapaxes(value_cache, 1, 2)
    far_k = hop(key_cache, "ctx", mate)
    far_v = hop(values_t, "ctx", mate)
    blocks, (table, dec_rows, norms) = gather_rows(hidden_in, (table, dec_rows, norms))
    q, new_keys, new_values, new_values_t, k_dec, v_dec, mlp_in = qkv(
        scal, blocks, dec_rows, norms, qkv_weight, qkv_bias, table, [far_k]
    )
    q_far = hop(q[: seqs * rows].reshape(seqs, rows, -1), "ctx", across)
    kv = (key_cache, values_t, new_keys, new_values_t)
    far_kv = (far_k, far_v, hop(new_keys, "ctx", mate), hop(new_values_t, "ctx", mate))

    up = up_proj(scal, mlp_in, up_weight, up_bias[None, :], [])
    own, far, last = [], [], [up, far_v]
    for s in range(seqs):
        own.append(attend_one(own_body, scal, s, q, kv, last))
        last = [own[s]]
    for s in range(seqs):
        far.append(attend_one(far_body, scal, s, q_far, kv, last))
        last = [far[s]]
    mlp = down_proj(scal, up, down_weight, last)
    last = [mlp]
    ends = []
    for s in range(seqs):
        mine, back = attend_second(scal, s, q, q_far, far_kv, own[s], far[s], last)
        last = [back]
        ends.append((mine, hop(back, "ctx", across)))
    dec = attend_dec(scal, q, kv, far_kv, last)
    dec_far = hop(dec, "ctx", across)
    attn_dec = decode_attn(scal, q, k_dec, v_dec, [dec, dec_far], [ends[-1][1]])
    last = attn_dec

    bias = lax.dynamic_slice_in_dim(out_bias + down_bias, me * part, part)
    prefill = []
    for s in range(seqs):
        odd, even = out_proj(
            scal, s, *ends[s], attn_dec if s == seqs - 1 else None, out_weight, mlp, [last]
        )
        last = even
        summed = scatter_rows(odd, even, rows)
        live = index < new_len[s]
        full = hidden_in[s].astype(F32) + summed[:rows] + bias
        prefill.append(jnp.where(live[:, None], full, 0.0).astype(BF))
        if s == seqs - 1:
            resid = lax.dynamic_slice_in_dim(decode_in, me * part, part, 1)
            decode_out = (resid.astype(F32) + summed[rows : rows + seqs] + bias).astype(BF)
    return (jnp.stack(prefill), new_keys, new_values, decode_out)


def layer(ctx, tp, *args):
    seqs, rows, part = args[0].shape
    pre, cols = args[4].shape[1:]
    if tp == 8 and ctx == 4 and seqs == 2 and rows % HD == 0 and pre % HD == 0 and cols == 4 * HD:
        return moved_queries(*args)
    return shards(*args)


def solution(mesh):
    return jax.shard_map(
        functools.partial(layer, mesh.shape["ctx"], mesh.shape["tp"]),
        mesh=mesh,
        in_specs=(
            P(None, "ctx", "tp"),
            P(),
            P(),
            P(),
            P(None, "ctx", "tp"),
            P(None, "ctx", "tp"),
            P(),
            P(),
            P(),
            P(),
            P(None, None, "tp"),
            P(None, "tp"),
            P("tp", None),
            P(),
            P(None, "tp"),
            P("tp"),
            P("tp", None),
            P(),
        ),
        out_specs=(P(None, "ctx", "tp"), P(None, "ctx", "tp"), P(None, "ctx", "tp"), P(None, "tp")),
        check_vma=False,
    )
```

```python
import functools
import math

import jax
import jax.numpy as jnp
from jax import lax
from jax.experimental import pallas as pl
from jax.experimental.pallas import tpu as pltpu
from jax.sharding import PartitionSpec as P

HD = 128
ROT = 32


EPS = 1e-05
NEG = -1e30


def joined_2(part, axis, combine):
    gathered = jax.tree.map(lambda a: lax.all_gather(a, axis), part)

    def take(source):
        return jax.tree.map(lambda a: lax.dynamic_index_in_dim(a, source, 0, False), gathered)

    return lax.fori_loop(
        1, lax.axis_size(axis), lambda source, state: combine(state, take(source)), take(0)
    )


def norm_rows(rows, gain, shift):
    values = rows.astype(jnp.float32)
    center = values - jnp.mean(values, axis=-1, keepdims=True)
    spread = jnp.mean(center * center, axis=-1, keepdims=True)
    return (center * lax.rsqrt(spread + EPS) * gain + shift).astype(jnp.bfloat16)


def rotate(values, position):
    half = ROT // 2
    freqs = jnp.exp(jnp.arange(half, dtype=jnp.float32) * (-2.0 * math.log(10000.0) / ROT))
    angle = position.astype(jnp.float32)[..., None] * freqs
    cosine = jnp.cos(angle)
    sine = jnp.sin(angle)
    first = values[..., :half]
    second = values[..., half:ROT]
    return jnp.concatenate(
        [first * cosine - second * sine, second * cosine + first * sine, values[..., ROT:]], axis=-1
    )


def key_status(first, count, pre_dev, new_dev, pre_len, new_len):
    index = first + jnp.arange(count, dtype=jnp.int32)
    owner = index // (pre_dev + new_dev)
    offset = index % (pre_dev + new_dev)
    is_prefix = offset < pre_dev
    prefix_pos = owner * pre_dev + offset
    new_pos = owner * new_dev + offset - pre_dev
    prefix_ok = is_prefix[None, :] & (prefix_pos[None, :] < pre_len[:, None])
    new_ok = jnp.logical_not(is_prefix)[None, :] & (new_pos[None, :] < new_len[:, None])
    return (prefix_ok, new_ok, new_pos)


def absorb(state, queries, keys, values, allowed):
    top, total, acc = state
    scores = jnp.einsum("sqhd,skhd->shqk", queries, keys, preferred_element_type=jnp.float32) * (
        1.0 / math.sqrt(HD)
    )
    mask = allowed[:, None]
    scores = jnp.where(mask, scores, NEG)
    new_top = jnp.maximum(top, jnp.max(scores, axis=-1))
    weight = jnp.where(mask, jnp.exp(scores - new_top[..., None]), 0.0)
    factor = jnp.exp(top - new_top)
    total = total * factor + jnp.sum(weight, axis=-1)
    acc = acc * factor[..., None] + jnp.einsum(
        "shqk,skhd->shqd", weight.astype(jnp.bfloat16), values, preferred_element_type=jnp.float32
    )
    return (new_top, total, acc)


def empty_state(seqs, heads_dev, count):
    return (
        jnp.full((seqs, heads_dev, count), NEG, jnp.float32),
        jnp.zeros((seqs, heads_dev, count), jnp.float32),
        jnp.zeros((seqs, heads_dev, count, HD), jnp.float32),
    )


def join_parts(first, second):
    best = jnp.maximum(first[0], second[0])
    left = jnp.exp(first[0] - best)
    right = jnp.exp(second[0] - best)
    return (
        best,
        first[1] * left + second[1] * right,
        first[2] * left[..., None] + second[2] * right[..., None],
    )


def shards(
    hidden_in,
    decode_in,
    pre_len,
    new_len,
    key_cache,
    value_cache,
    ln_attn_gain,
    ln_attn_bias,
    ln_mlp_gain,
    ln_mlp_bias,
    qkv_weight,
    qkv_bias,
    out_weight,
    out_bias,
    up_weight,
    up_bias,
    down_weight,
    down_bias,
):
    seqs, new_dev, part_cols = hidden_in.shape
    pre_dev = key_cache.shape[1]
    local_cols = qkv_weight.shape[2]
    heads_dev = local_cols // HD
    width = decode_in.shape[1]
    block_len = pre_dev + new_dev
    rows_new = seqs * new_dev
    ctx_rank = lax.axis_index("ctx")
    tp_rank = lax.axis_index("tp")
    whole = lax.all_gather(hidden_in, "tp", axis=2, tiled=True)
    joined = jnp.concatenate([whole.reshape(rows_new, width), decode_in], axis=0)
    attn_in = norm_rows(joined, ln_attn_gain, ln_attn_bias)
    mlp_in = norm_rows(joined, ln_mlp_gain, ln_mlp_bias)
    proj = [
        jnp.dot(attn_in, qkv_weight[i], preferred_element_type=jnp.float32) + qkv_bias[i]
        for i in range(3)
    ]
    up_act = jax.nn.gelu(
        jnp.dot(mlp_in, up_weight, preferred_element_type=jnp.float32) + up_bias, approximate=False
    ).astype(jnp.bfloat16)
    query_index = ctx_rank * new_dev + jnp.arange(new_dev, dtype=jnp.int32)
    position = pre_len[:, None] + query_index[None, :]
    dec_position = pre_len + new_len
    q_new = rotate(
        proj[0][:rows_new].reshape(seqs, new_dev, heads_dev, HD), position[..., None]
    ).astype(jnp.bfloat16)
    k_new = rotate(
        proj[1][:rows_new].reshape(seqs, new_dev, heads_dev, HD), position[..., None]
    ).astype(jnp.bfloat16)
    v_new = proj[2][:rows_new].reshape(seqs, new_dev, heads_dev, HD).astype(jnp.bfloat16)
    q_dec = rotate(proj[0][rows_new:].reshape(seqs, heads_dev, HD), dec_position[:, None]).astype(
        jnp.bfloat16
    )
    k_dec = rotate(proj[1][rows_new:].reshape(seqs, heads_dev, HD), dec_position[:, None]).astype(
        jnp.bfloat16
    )
    v_dec = proj[2][rows_new:].reshape(seqs, heads_dev, HD).astype(jnp.bfloat16)
    live = query_index[None, :] < new_len[:, None]
    flat_keys = k_new.reshape(seqs, new_dev, local_cols)
    flat_values = v_new.reshape(seqs, new_dev, local_cols)
    new_keys = jnp.where(live[..., None], flat_keys, 0)
    new_values = jnp.where(live[..., None], flat_values, 0)
    local_block = jnp.concatenate(
        [jnp.stack([key_cache, value_cache], axis=2), jnp.stack([flat_keys, flat_values], axis=2)],
        axis=1,
    )
    local_keys = local_block[:, :, 0].reshape(seqs, block_len, heads_dev, HD)
    local_values = local_block[:, :, 1].reshape(seqs, block_len, heads_dev, HD)

    def allowed_for(first, count, queries_at):
        prefix_ok, new_ok, new_pos = key_status(first, count, pre_dev, new_dev, pre_len, new_len)
        return prefix_ok[:, None, :] | new_ok[:, None, :] & (
            new_pos[None, None, :] <= queries_at[None, :, None]
        )

    state = empty_state(seqs, heads_dev, new_dev)
    piece = lax.all_gather(local_block, "ctx", axis=1, tiled=True)
    blocks = piece.shape[1] // block_len

    def one_block(inner, number):
        begin = number * block_len
        slab = lax.dynamic_slice_in_dim(piece, begin, block_len, 1)
        keys = slab[:, :, 0].reshape(seqs, block_len, heads_dev, HD)
        values = slab[:, :, 1].reshape(seqs, block_len, heads_dev, HD)
        allowed = allowed_for(begin, block_len, query_index)
        return (absorb(inner, q_new, keys, values, allowed), None)

    state, _ = lax.scan(one_block, state, jnp.arange(blocks, dtype=jnp.int32))
    top, total, acc = state
    attn_new = (
        (acc / total[..., None])
        .transpose(0, 2, 1, 3)
        .reshape(rows_new, local_cols)
        .astype(jnp.bfloat16)
    )
    prefix_ok, new_ok, new_pos = key_status(
        ctx_rank * block_len, block_len, pre_dev, new_dev, pre_len, new_len
    )
    dec_allowed = (prefix_ok | new_ok)[:, None, :]
    dec_state = absorb(
        empty_state(seqs, heads_dev, 1), q_dec[:, None], local_keys, local_values, dec_allowed
    )
    dec_top, dec_total, dec_acc = joined_2(dec_state, "ctx", join_parts)
    dec_top = dec_top[..., 0]
    dec_total = dec_total[..., 0]
    dec_acc = dec_acc[:, :, 0]
    own = jnp.einsum("shd,shd->sh", q_dec, k_dec, preferred_element_type=jnp.float32) * (
        1.0 / math.sqrt(HD)
    )
    best = jnp.maximum(dec_top, own)
    far_factor = jnp.exp(dec_top - best)
    own_weight = jnp.exp(own - best)
    dec_total = dec_total * far_factor + own_weight
    dec_acc = dec_acc * far_factor[..., None] + jnp.einsum(
        "sh,shd->shd", own_weight.astype(jnp.bfloat16), v_dec, preferred_element_type=jnp.float32
    )
    attn_dec = (dec_acc / dec_total[..., None]).reshape(seqs, local_cols).astype(jnp.bfloat16)
    attn_rows = jnp.concatenate([attn_new, attn_dec], axis=0)
    branches = jnp.dot(attn_rows, out_weight, preferred_element_type=jnp.float32) + jnp.dot(
        up_act, down_weight, preferred_element_type=jnp.float32
    )
    summed_new, summed_dec = (
        lax.psum_scatter(
            branches[:rows_new].reshape(seqs, new_dev, width).astype(jnp.bfloat16),
            "tp",
            scatter_dimension=2,
            tiled=True,
        ).astype(jnp.float32),
        lax.psum_scatter(
            branches[rows_new:].astype(jnp.bfloat16), "tp", scatter_dimension=1, tiled=True
        ).astype(jnp.float32),
    )
    bias = lax.dynamic_slice_in_dim(out_bias + down_bias, tp_rank * part_cols, part_cols)
    prefill = hidden_in.astype(jnp.float32) + summed_new + bias
    prefill_out = jnp.where(live[..., None], prefill, 0.0).astype(jnp.bfloat16)
    dec_resid = lax.dynamic_slice_in_dim(decode_in, tp_rank * part_cols, part_cols, 1)
    decode_out = (dec_resid.astype(jnp.float32) + summed_dec + bias).astype(jnp.bfloat16)
    return (prefill_out, new_keys, new_values, decode_out)


BF = jnp.bfloat16
F32 = jnp.float32
DEC = 16
LSE = 16
SCALE = 1.0 / math.sqrt(HD)


def hop(value, axis, pairs):
    return lax.ppermute(value, axis, pairs)


def call(body, scal, ins, outs, scratch=(), limit=16, after=(), left=()):
    n, m = 1 + len(ins), len(after)
    left = [pltpu.with_memory_space_constraint(a, pltpu.HBM) for a in left]

    def run(*refs):
        body(*refs[: n + len(left)], *refs[n + len(left) + m :])

    return pl.pallas_call(
        run,
        out_shape=outs,
        in_specs=[pl.BlockSpec(memory_space=pltpu.SMEM)]
        + [pl.BlockSpec(memory_space=pltpu.VMEM)] * len(ins)
        + [pl.BlockSpec(memory_space=pltpu.HBM)] * len(left)
        + [pl.BlockSpec(memory_space=pl.ANY)] * m,
        out_specs=jax.tree.map(lambda _: pl.BlockSpec(memory_space=pltpu.VMEM), outs),
        scratch_shapes=list(scratch),
        compiler_params=pltpu.CompilerParams(vmem_limit_bytes=limit << 20),
    )(scal, *ins, *left, *after)


def struct(shape, dtype):
    return jax.ShapeDtypeStruct(tuple(shape), dtype)


ME, RANK, PRE, NEW = 0, 1, 2, 2 + DEC


def turn(values, table):
    cosine, down, up = (table[i] for i in range(3))
    parts = []
    for h in range(values.shape[1] // HD):
        one = values[:, h * HD : (h + 1) * HD]
        parts.append(
            one * cosine
            + pltpu.roll(one, HD - ROT // 2, 1) * down
            + pltpu.roll(one, ROT // 2, 1) * up
        )
    return jnp.concatenate(parts, axis=1)


def qkv_body(seqs, rows, part, sc, dec, norms, bias, table, *refs):
    weight, blocks = refs[0], refs[1:11]
    q_out, keys, values, values_t, k_dec, v_dec, mlp_in = refs[11:18]
    attn_in, held, hidden, sems, block_sems = refs[18:]
    moves = []
    for s in range(seqs):
        sources = [blocks[k].at[s] for k in range(6)] + [blocks[6 + s], blocks[8 + s]]
        moves.append(
            [
                pltpu.make_async_copy(source, hidden.at[s, k], block_sems.at[s, k])
                for k, source in enumerate(sources)
            ]
        )
        for move in moves[s]:
            move.start()
    copies = [pltpu.make_async_copy(weight.at[i], held.at[i], sems.at[i]) for i in range(3)]
    for copy in copies:
        copy.start()
    me = sc[ME]
    width = part * 8

    def finish(values, base, count, cols):
        total = functools.reduce(lambda a, b: a + b, values)
        mean = jnp.sum(total, axis=-1, keepdims=True) * (1.0 / width)
        values = [v - mean for v in values]
        square = functools.reduce(lambda a, b: a + b, [v * v for v in values])
        spread = jnp.sum(square, axis=-1, keepdims=True) * (1.0 / width)
        inv = lax.rsqrt(spread + EPS)
        for v, col in zip(values, cols, strict=True):
            v = v * inv
            at = pl.ds(col, part)
            attn_in[pl.ds(base, count), at] = (
                v * norms[pl.ds(0, 1), at] + norms[pl.ds(1, 1), at]
            ).astype(BF)
            mlp_in[pl.ds(base, count), at] = (
                v * norms[pl.ds(2, 1), at] + norms[pl.ds(3, 1), at]
            ).astype(BF)

    cols = [pl.multiple_of((me ^ k) * part, part) for k in range(8)]
    for s in range(seqs):
        for move in moves[s]:
            move.wait()

        def step(i, carry):
            at = pl.multiple_of(i * 16, 16)
            rows_of = [hidden[s, k, pl.ds(at, 16), :].astype(F32) for k in range(8)]
            finish(rows_of, pl.multiple_of(s * rows + at, 16), 16, cols)
            return carry

        lax.fori_loop(0, rows // 16, step, 0, unroll=4)
    tokens = [dec[:, pl.ds(k * part, part)].astype(F32) for k in range(8)]
    finish(tokens, seqs * rows, DEC, [k * part for k in range(8)])
    first = sc[RANK] * rows
    slot = lax.broadcasted_iota(jnp.int32, (rows, 1), 0) + first
    outs = []
    for i in range(3):
        copies[i].wait()
        out = jnp.dot(attn_in[...], held[i], preferred_element_type=F32) + bias[pl.ds(i, 1), :]
        if i < 2:
            out = turn(out, table)
        if i == 0:
            q_out[...] = out.astype(BF)
            continue
        for s in range(seqs):
            one = jnp.where(slot < sc[NEW + s], out[s * rows : (s + 1) * rows], 0.0)
            (keys if i == 1 else values)[s] = one.astype(BF)
            if i == 2:
                values_t[s] = jnp.transpose(one).astype(BF)
        (k_dec if i == 1 else v_dec)[...] = out[seqs * rows :].astype(BF)


def qkv(scal, blocks, dec, norms, weight, bias, table, after):
    seqs, rows, part = blocks[0].shape
    _, width, cols = weight.shape
    total = seqs * rows + DEC
    return call(
        functools.partial(qkv_body, seqs, rows, part),
        scal,
        [dec, norms, bias, table],
        (
            struct((total, cols), BF),
            *[struct((seqs, rows, cols), BF)] * 2,
            struct((seqs, cols, rows), BF),
            *[struct((DEC, cols), BF)] * 2,
            struct((total, width), BF),
        ),
        scratch=[
            pltpu.VMEM((total, width), BF),
            pltpu.VMEM((3, width, cols), BF),
            pltpu.VMEM((seqs, 8, rows, part), BF),
            pltpu.SemaphoreType.DMA((3,)),
            pltpu.SemaphoreType.DMA((seqs, 8)),
        ],
        limit=32,
        left=[weight, *blocks],
        after=after,
    )


def attend(query, pieces):
    scores = []
    for keys, _, limit in pieces:
        s = lax.dot_general(query, keys, (((1,), (1,)), ((), ())), preferred_element_type=F32)
        col = lax.broadcasted_iota(jnp.int32, s.shape, 1)
        scores.append(jnp.where(col < limit, s, NEG))
    top = functools.reduce(jnp.maximum, [jnp.max(s, axis=-1, keepdims=True) for s in scores])
    total = 0.0
    acc = 0.0
    for s, (_, values_t, _) in zip(scores, pieces, strict=True):
        weight = jnp.exp2((s - top) * (SCALE * math.log2(math.e)))
        total = total + jnp.sum(weight, axis=-1, keepdims=True)
        acc = acc + lax.dot_general(
            weight.astype(BF), values_t, (((1,), (1,)), ((), ())), preferred_element_type=F32
        )
    return acc / total, top * SCALE + jnp.log(total)


def attend_t(query, pieces):
    scores = []
    for keys, _, limit in pieces:
        s = lax.dot_general(keys, query, (((1,), (1,)), ((), ())), preferred_element_type=F32)
        row = lax.broadcasted_iota(jnp.int32, s.shape, 0)
        scores.append(jnp.where(row < limit, s, NEG))
    top = functools.reduce(jnp.maximum, [jnp.max(s, axis=0, keepdims=True) for s in scores])
    total = 0.0
    acc = 0.0
    for s, (_, values_t, _) in zip(scores, pieces, strict=True):
        weight = jnp.exp2((s - top) * (SCALE * math.log2(math.e)))
        total = total + jnp.sum(weight, axis=0, keepdims=True)
        acc = acc + jnp.dot(values_t, weight.astype(BF), preferred_element_type=F32)
    return acc / total, top * SCALE + jnp.log(total)


def pack_logs(logs):
    logs = jnp.concatenate(logs, axis=0)
    pieces = []
    for _ in range(3):
        short = logs.astype(BF).astype(F32)
        pieces.append(short)
        logs = logs - short
    return jnp.concatenate(pieces + [jnp.zeros_like(logs)], axis=0).astype(BF)


def unpack_logs(tile):
    tile = tile.astype(F32)
    return (tile[0:4] + tile[4:8]) + tile[8:12]


def head_slices(cols):
    return [slice(h * HD, (h + 1) * HD) for h in range(cols // HD)]


def attend_all(q, kc, vc, kn, vn, pre, new):
    found = []
    for at in head_slices(q.shape[1]):
        pieces = [(kc[:, at], vc[at, :], pre), (kn[:, at], vn[at, :], new)]
        found.append(attend_t(q[:, at], pieces))
    return found


def store_partial(out, heads, logs):
    cols = out.shape[0] - LSE
    for at, head in zip(head_slices(cols), heads, strict=True):
        out[at, :] = head.astype(BF)
    out[pl.ds(cols, LSE), :] = pack_logs(logs)


def limits(sc, seq, owner, asker, pre, rows):
    cached = sc[PRE + seq] - owner * pre
    col = lax.broadcasted_iota(jnp.int32, (1, rows), 1)
    fresh = jnp.minimum(sc[NEW + seq] - owner * rows, (asker - owner) * rows + col + 1)
    return cached, fresh


def own_body(seq, rows, pre, sc, q, kc, vc, kn, vn, out):
    rank = sc[RANK]
    found = attend_all(
        q.at[pl.ds(seq * rows, rows)],
        *(a.at[seq] for a in (kc, vc, kn, vn)),
        *limits(sc, seq, rank, rank, pre, rows),
    )
    store_partial(out, *zip(*found, strict=True))


def far_body(seq, rows, pre, sc, q, kc, vc, kn, vn, out):
    rank = sc[RANK]
    found = attend_all(
        q.at[seq],
        *(a.at[seq] for a in (kc, vc, kn, vn)),
        *limits(sc, seq, rank, rank ^ 3, pre, rows),
    )
    store_partial(out, *zip(*found, strict=True))


def attend_one(body, scal, seq, q, kv, after):
    pre, cols = kv[0].shape[1:]
    rows = kv[2].shape[1]
    return call(
        functools.partial(body, seq, rows, pre),
        scal,
        [q, *kv],
        struct((cols + LSE, rows), BF),
        after=after,
    )


def second_body(seq, rows, pre, sc, q, q_far, kc, vc, kn, vn, mine, mine_far, out, out_far):
    rank = sc[RANK]
    cols = kc.shape[2]
    for asker, source, before, target in (
        (rank ^ 3, q_far.at[seq], mine_far, out_far),
        (rank, q.at[pl.ds(seq * rows, rows)], mine, out),
    ):
        found = attend_all(
            source,
            kc.at[seq],
            vc.at[seq],
            kn,
            vn,
            *limits(sc, seq, rank ^ 1, asker, pre, rows),
        )
        earlier = unpack_logs(before[pl.ds(cols, LSE), :])
        heads, logs = [], []
        for h, at in enumerate(head_slices(cols)):
            head, log = found[h]
            old = earlier[h : h + 1]
            top = jnp.maximum(log, old)
            a, b = jnp.exp(log - top), jnp.exp(old - top)
            total = a + b
            heads.append((a / total) * head + (b / total) * before[at, :].astype(F32))
            logs.append(top + jnp.log(total))
        store_partial(target, heads, logs)


def attend_second(scal, seq, q, q_far, kv, mine, mine_far, after):
    pre, cols = kv[0].shape[1:]
    rows = kv[2].shape[0]
    return call(
        functools.partial(second_body, seq, rows, pre),
        scal,
        [q, q_far, *kv, mine, mine_far],
        (struct((cols + LSE, rows), BF),) * 2,
        after=after,
    )


def dec_body(seqs, rows, pre, sc, q, kc, vc, kn, vn, *refs):
    far, out = refs[:-1], refs[-1]
    far = [(far[0].at[s], far[1].at[s], far[2 + 2 * s], far[3 + 2 * s]) for s in range(seqs)]
    rank = sc[RANK]
    row = lax.broadcasted_iota(jnp.int32, (DEC, 1), 0)
    for at in head_slices(kc.shape[2]):
        result = jnp.zeros((DEC, HD), F32)
        log = jnp.full((DEC, HD), NEG, F32)
        for s in range(seqs):
            pieces = []
            mine = (kc.at[s], vc.at[s], kn.at[s], vn.at[s])
            for owner, (k, v, k2, v2) in ((rank, mine), (rank ^ 1, far[s])):
                pieces.append((k[:, at], v[at, :], sc[PRE + s] - owner * pre))
                pieces.append((k2[:, at], v2[at, :], sc[NEW + s] - owner * rows))
            one, one_log = attend(q[pl.ds(seqs * rows, DEC), at], pieces)
            result = jnp.where(row == s, one, result)
            log = jnp.where(row == s, jnp.broadcast_to(one_log, (DEC, HD)), log)
        out[pl.ds(0, DEC), at] = result
        out[pl.ds(DEC, DEC), at] = log


def attend_dec(scal, q, kv, far, after):
    seqs, pre, cols = kv[0].shape
    rows = kv[2].shape[1]
    return call(
        functools.partial(dec_body, seqs, rows, pre),
        scal,
        [q, *kv, *far],
        struct((2 * DEC, cols), F32),
        after=after,
    )


def blend(parts):
    cols = parts[0].shape[0] - LSE
    logs = [unpack_logs(ref[pl.ds(cols, LSE), :]) for ref in parts]
    top = functools.reduce(jnp.maximum, logs)
    weights = [jnp.exp(log - top) for log in logs]
    total = functools.reduce(lambda x, y: x + y, weights)
    heads = []
    for h, at in enumerate(head_slices(cols)):
        acc = 0.0
        for w, ref in zip(weights, parts, strict=True):
            acc = acc + (w / total)[h : h + 1] * ref[at, :].astype(F32)
        heads.append(acc)
    return heads


def decode_body(n, base, sc, q, k, v, *refs):
    parts, out = refs[:n], refs[n]
    for at in head_slices(k.shape[1]):
        both = q[pl.ds(base, DEC), at].astype(F32) * k[:, at].astype(F32)
        own = jnp.broadcast_to(jnp.sum(both, axis=-1, keepdims=True) * SCALE, (DEC, HD))
        logs = [p[pl.ds(DEC, DEC), at] for p in parts]
        top = functools.reduce(jnp.maximum, logs, own)
        share = jnp.exp(own - top)
        total = share
        acc = share.astype(BF).astype(F32) * v[:, at].astype(F32)
        for p, log in zip(parts, logs, strict=True):
            share = jnp.exp(log - top)
            total = total + share
            acc = acc + share * p[pl.ds(0, DEC), at]
        out[:, at] = (acc / total).astype(BF)


def decode_attn(scal, q, k_dec, v_dec, parts, after):
    return call(
        functools.partial(decode_body, len(parts), q.shape[0] - DEC),
        scal,
        [q, k_dec, v_dec, *parts],
        struct(k_dec.shape, BF),
        after=after,
    )


def fetch(weight, held, sems, tile):
    copies = []
    for i in range(weight.shape[1] // tile):
        at = (slice(None), pl.ds(i * tile, tile))
        copies.append(pltpu.make_async_copy(weight.at[at], held.at[at], sems.at[i]))
    for copy in copies:
        copy.start()
    return copies


def up_body(tile, sc, x, bias, weight, out, held, sems):
    fetch(weight, held, sems, tile)

    def step(i, carry):
        at = (slice(None), pl.ds(pl.multiple_of(i * tile, tile), tile))
        pltpu.make_async_copy(weight.at[at], held.at[at], sems.at[i]).wait()
        y = jnp.dot(x[...], held[at], preferred_element_type=F32) + bias[at]
        out[at] = (0.5 * y * (1.0 + lax.erf(y * math.sqrt(0.5)))).astype(BF)
        return carry

    lax.fori_loop(0, weight.shape[1] // tile, step, 0)


def up_proj(scal, x, weight, bias, after):
    total = x.shape[0]
    width, units = weight.shape
    tile = 512
    return call(
        functools.partial(up_body, tile),
        scal,
        [x, bias],
        struct((total, units), BF),
        scratch=[pltpu.VMEM(weight.shape, BF), pltpu.SemaphoreType.DMA((units // tile,))],
        limit=24,
        left=[weight],
        after=after,
    )


def down_body(tile, sc, x, weight, out, held, sems):
    for i, copy in enumerate(fetch(weight, held, sems, tile)):
        copy.wait()
        at = slice(i * tile, (i + 1) * tile)
        out[:, at] = jnp.dot(x[...], held[:, at], preferred_element_type=F32).astype(BF)


def down_proj(scal, x, weight, after):
    total = x.shape[0]
    units, width = weight.shape
    tile = 1024
    return call(
        functools.partial(down_body, tile),
        scal,
        [x],
        struct((total, width), BF),
        scratch=[pltpu.VMEM(weight.shape, BF), pltpu.SemaphoreType.DMA((width // tile,))],
        limit=24,
        left=[weight],
        after=after,
    )


def place(k):
    return (7 - k) // 2


def out_body(seq, tail, rows, part, sc, mine, far, *refs):
    if tail:
        dec, refs = refs[0], refs[1:]
    weight, mlp, odd, even, attn = refs
    for at, head in zip(head_slices(attn.shape[1]), blend([mine, far]), strict=True):
        attn[pl.ds(0, rows), at] = jnp.transpose(head).astype(BF)
    if tail:
        attn[pl.ds(rows, DEC), :] = dec[...]
    for j in range(8):
        k = sc[ME] ^ j
        at = slice(j * part, (j + 1) * part)
        out = jnp.dot(attn[...], weight[:, at], preferred_element_type=F32)
        base = mlp[pl.ds(seq * rows, rows), at].astype(F32)
        if tail:
            base = jnp.concatenate([base, mlp[pl.ds(mlp.shape[0] - DEC, DEC), at].astype(F32)], axis=0)
        out = (out + base).astype(BF)

        @pl.when(k % 2 == 1)
        def _():
            odd[place(k)] = out

        @pl.when(k % 2 == 0)
        def _():
            even[place(k)] = out


def out_proj(scal, seq, mine, far, dec, weight, mlp, after):
    cols, width = weight.shape
    rows = mine.shape[1]
    part = width // 8
    tail = dec is not None
    total = rows + (DEC if tail else 0)
    return call(
        functools.partial(out_body, seq, tail, rows, part),
        scal,
        [mine, far] + ([dec] if tail else []) + [weight, mlp],
        (struct((4, total, part), BF),) * 2,
        scratch=[pltpu.VMEM((total, cols), BF)],
        after=after,
    )


def swap(value, bit):
    return hop(value, "tp", [(i, i ^ bit) for i in range(8)])


def gather_rows(own, beside):
    x, y, c = swap(own, 2), swap(own, 4), swap(own, 1)
    x, y, beside = lax.optimization_barrier((x, y, beside))
    da, db = swap(y[0], 2), swap(x[1], 4)
    cx, cy = swap(x, 1), swap(y, 1)
    ca, cb = swap(da, 1), swap(db, 1)
    return [own, c, x, cx, y, cy, da, db, ca, cb], beside


def scatter_rows(odd, even, rows):
    half = rows // 2

    def both(a, b):
        return a.astype(F32) + b.astype(F32)

    other = swap(odd, 1)
    far = both(even[0], other[0]).astype(BF)
    got_y, got_x = swap(far[:half], 2), swap(far[half:], 4)
    to_y = both(even[1], other[1])
    to_y = jnp.concatenate([to_y[:half] + got_y.astype(F32), to_y[half:]], axis=0).astype(BF)
    to_x = both(even[2], other[2])
    to_x = jnp.concatenate([to_x[:half], to_x[half:] + got_x.astype(F32)], axis=0).astype(BF)
    from_x, from_y = swap(to_x, 2), swap(to_y, 4)
    return both(even[3], other[3]) + both(from_x, from_y)


def rope_table(position):
    lane = jnp.arange(HD, dtype=jnp.int32)
    half = ROT // 2
    freqs = jnp.exp((lane % half).astype(F32) * (-2.0 * math.log(10000.0) / ROT))
    angle = position.astype(F32)[:, None] * freqs[None, :]
    cosine = jnp.where(lane < ROT, jnp.cos(angle), 1.0)
    sine = jnp.sin(angle)
    down = jnp.where(lane < half, -sine, 0.0)
    up = jnp.where((lane >= half) & (lane < ROT), sine, 0.0)
    return jnp.stack([cosine, down, up])


def moved_queries(
    hidden_in,
    decode_in,
    pre_len,
    new_len,
    key_cache,
    value_cache,
    ln_attn_gain,
    ln_attn_bias,
    ln_mlp_gain,
    ln_mlp_bias,
    qkv_weight,
    qkv_bias,
    out_weight,
    out_bias,
    up_weight,
    up_bias,
    down_weight,
    down_bias,
):
    seqs, rows, part = hidden_in.shape
    n = lax.axis_size("ctx")
    rank = lax.axis_index("ctx")
    me = lax.axis_index("tp")
    mate = [(i, i ^ 1) for i in range(n)]
    across = [(i, i ^ 3) for i in range(n)]
    room = (0, DEC - seqs)
    scal = jnp.concatenate([jnp.stack([me, rank]), jnp.pad(pre_len, room), jnp.pad(new_len, room)])
    norms = jnp.stack([ln_attn_gain, ln_attn_bias, ln_mlp_gain, ln_mlp_bias])
    dec_rows = jnp.pad(decode_in, (room, (0, 0)))
    index = rank * rows + jnp.arange(rows, dtype=jnp.int32)
    position = [pre_len[s] + index for s in range(seqs)] + [jnp.pad(pre_len + new_len, room)]
    table = rope_table(jnp.concatenate(position))

    values_t = jnp.swapaxes(value_cache, 1, 2)
    far_k = hop(key_cache, "ctx", mate)
    far_v = hop(values_t, "ctx", mate)
    blocks, (table, dec_rows, norms) = gather_rows(hidden_in, (table, dec_rows, norms))
    q, new_keys, new_values, new_values_t, k_dec, v_dec, mlp_in = qkv(
        scal, blocks, dec_rows, norms, qkv_weight, qkv_bias, table, [far_k]
    )
    q_far = hop(q[: seqs * rows].reshape(seqs, rows, -1), "ctx", across)
    kv = (key_cache, values_t, new_keys, new_values_t)
    pairs = [
        (far_k, far_v, hop(new_keys[s], "ctx", mate), hop(new_values_t[s], "ctx", mate))
        for s in range(seqs)
    ]

    up = up_proj(scal, mlp_in, up_weight, up_bias[None, :], [])
    own, far, last = [], [], [up, far_v]
    for s in range(seqs):
        own.append(attend_one(own_body, scal, s, q, kv, last))
        last = [own[s]]
    for s in range(seqs):
        far.append(attend_one(far_body, scal, s, q_far, kv, last))
        last = [far[s]]
    last.append(pairs[1][2])
    ends = []
    for s in range(seqs):
        mine, back = attend_second(scal, s, q, q_far, pairs[s], own[s], far[s], last)
        last = [back]
        ends.append((mine, hop(back, "ctx", across)))
        if s == 0:
            mlp = down_proj(scal, up, down_weight, [back, pairs[1][3]])
            last = [mlp]
    dec = attend_dec(scal, q, kv, [*pairs[0], *pairs[1][2:]], last)
    dec_far = hop(dec, "ctx", across)
    attn_dec = decode_attn(scal, q, k_dec, v_dec, [dec, dec_far], [ends[-1][1]])
    last = attn_dec

    bias = lax.dynamic_slice_in_dim(out_bias + down_bias, me * part, part)
    prefill = []
    for s in range(seqs):
        odd, even = out_proj(
            scal, s, *ends[s], attn_dec if s == seqs - 1 else None, out_weight, mlp, [last]
        )
        last = even
        summed = scatter_rows(odd, even, rows)
        live = index < new_len[s]
        full = hidden_in[s].astype(F32) + summed[:rows] + bias
        prefill.append(jnp.where(live[:, None], full, 0.0).astype(BF))
        if s == seqs - 1:
            resid = lax.dynamic_slice_in_dim(decode_in, me * part, part, 1)
            decode_out = (resid.astype(F32) + summed[rows : rows + seqs] + bias).astype(BF)
    return (jnp.stack(prefill), new_keys, new_values, decode_out)


def layer(ctx, tp, *args):
    seqs, rows, part = args[0].shape
    pre, cols = args[4].shape[1:]
    if tp == 8 and ctx == 4 and seqs == 2 and rows % HD == 0 and pre % HD == 0 and cols == 4 * HD:
        return moved_queries(*args)
    return shards(*args)


def solution(mesh):
    return jax.shard_map(
        functools.partial(layer, mesh.shape["ctx"], mesh.shape["tp"]),
        mesh=mesh,
        in_specs=(
            P(None, "ctx", "tp"),
            P(),
            P(),
            P(),
            P(None, "ctx", "tp"),
            P(None, "ctx", "tp"),
            P(),
            P(),
            P(),
            P(),
            P(None, None, "tp"),
            P(None, "tp"),
            P("tp", None),
            P(),
            P(None, "tp"),
            P("tp"),
            P("tp", None),
            P(),
        ),
        out_specs=(P(None, "ctx", "tp"), P(None, "ctx", "tp"), P(None, "ctx", "tp"), P(None, "tp")),
        check_vma=False,
    )
```
